128 devices in a mesh: group: 8 (over y, core), dev: 16 (over z, x).
Axes of the slice: x: 4, y: 4, z: 4, core: 2. Of those that a mesh axis runs over, the one named last changes fastest.
Arguments:
- primary_q: bfloat16 [256, 3584, 1024], P(('group', 'dev')), may hold values from -0.09375 to 0.09375
- primary_scales: bfloat16 [256, 28, 8], P(('group', 'dev')), may hold values from 0.5 to 2
- new_place: int32 [128], P(('group', 'dev')), may hold values from 0 to 255, as said below
- tokens: bfloat16 [2048, 3584], P(('group', 'dev')), may hold values from -6 to 6
- experts: int32 [2048, 8], P(('group', 'dev')), may hold values from 0 to 255, all different within a row
- replica: int32 [2048, 8], P(('group', 'dev')), may hold values from 0 to 1
- route_num: int32 [2048, 8], P(('group', 'dev')), may hold values from 1 to 16
Outputs:
- new_weights: bfloat16 [128, 3584, 1024], P(('group', 'dev'))
- new_scales: bfloat16 [128, 28, 8], P(('group', 'dev'))
- hidden_out: bfloat16 [2048, 8, 1024], P(('group', 'dev'))
- slot_load: int32 [128, 3], P(('group', 'dev'))
The draws below stay inside these ranges and needn't reach their ends.
Inputs may be any that keep to these rules, and one draw needn't show every extreme that they name: `new_place`: the redundant slots of the 16 devices of one group hold 16 different experts, each with its primary copy on a device of that group.
All inputs are finite; a program needn't handle non-finite values.
Results may differ from the reference program's by a relative error of at most 0.0057.
Values may be sent and summed in bfloat16 or wider, within the bound.
A program may use at most 192 MiB of HBM per device.

```python
import math
import jax
import jax.numpy as jnp
from jax import lax

D = 3584
FF = 1024
TILE = 128
EXP_DEV = 2
TOPK = 8
CAP = 2
ROWS_DEV = 16
EXPERTS = 256
ROWS = 2048
N_GROUP = 8
N_DEV = 16


def draw_new_place(key, part):
    group_keys = jax.random.split(jax.random.fold_in(key, 17), N_GROUP)

    def one_group(group_key, group_id):
        chosen = jax.random.permutation(group_key, EXP_DEV * N_DEV)[:N_DEV]
        return chosen + group_id * EXP_DEV * N_DEV
    placed = jax.vmap(one_group)(group_keys, jnp.arange(N_GROUP, dtype=jnp.int32))
    return placed.reshape(N_GROUP * N_DEV).astype(jnp.int32)


def plant(array, stream_key, low, high):
    longest = array.shape.index(max(array.shape))
    spots = []
    for shift in (0, 1):
        where = [jax.random.randint(jax.random.fold_in(stream_key, axis), (), 0, length) for axis, length in enumerate(array.shape)]
        where[longest] = (where[longest] + shift) % array.shape[longest]
        spots.append(tuple(where))
    return array.at[spots[0]].set(low).at[spots[1]].set(high)


def levels(own_key, shape, shards, smallest, largest):
    gain, own = 1.0, jax.random.fold_in(own_key, 6)
    for dim, blocks in shards:
        steps = jnp.exp(jax.random.uniform(jax.random.fold_in(own, dim), (blocks,), jnp.float32, smallest / len(shards), largest / len(shards)))
        gain = gain * jnp.repeat(steps, shape[dim] // blocks).reshape([-1 if axis == dim else 1 for axis in range(len(shape))])
    return gain


def distinct(key, rows, number_of, top, lift):
    ranking = jax.random.permutation(jax.random.fold_in(key, 1), number_of)
    favour = ranking
    for power in range(3):
        favour = favour * favour // number_of
    favour = favour * lift // number_of
    chance = jax.random.randint(jax.random.fold_in(key, 2), (rows, number_of), 0, 4096) + favour
    holders = jax.random.permutation(jax.random.fold_in(key, 3), rows)[jnp.arange(number_of) % rows]
    chance = jnp.where(jnp.arange(rows)[:, None] == holders[None, :], 1 << 14, chance)
    merit = chance * number_of + jnp.arange(number_of)
    return lax.top_k(merit.astype(jnp.int32), top)[1].astype(jnp.int32)


def bell_draw(rng, shape, deviation, most, cuts=(), kind=jnp.bfloat16):
    result = jax.random.normal(rng, shape, jnp.float32) * deviation
    if len(cuts) > 0:
        result = levels(rng, shape, cuts, -0.22, 0.18) * result
    return jnp.clip(result, min=-most, max=most).astype(kind)


def setup_inputs(seed: int = 0) -> dict:
    arg_keys = jax.random.split(jax.random.key(seed), 8)
    return {
        "primary_q": bell_draw(arg_keys[0], (EXPERTS, D, FF), D ** -0.5, 0.09375, ((0, 128),)),
        "primary_scales": jnp.clip(jnp.exp(math.log(2.0) - 1.3862944 * jax.random.uniform(arg_keys[1], (EXPERTS, D // TILE, FF // TILE), jnp.float32) ** levels(arg_keys[1], (EXPERTS, D // TILE, FF // TILE), ((0, 128),), -0.2, 0.2)), 0.5, 2.0).astype(jnp.bfloat16),
        "new_place": draw_new_place(jax.random.fold_in(arg_keys[7], 71), 0),
        "tokens": bell_draw(arg_keys[3], (ROWS, D), 1.0, 6.0, ((0, 128),)),
        "experts": distinct(arg_keys[4], ROWS, EXPERTS, TOPK, 512),
        "replica": plant(jax.random.randint(arg_keys[5], (ROWS, TOPK), 0, 2), jax.random.fold_in(arg_keys[5], 1), 0, 1).astype(jnp.int32),
        "route_num": plant(jax.random.randint(arg_keys[6], (ROWS, TOPK), 1, 17), jax.random.fold_in(arg_keys[6], 1), 1, 16).astype(jnp.int32),
    }


def dequantize(values, scales):
    tile_grid = values.astype(jnp.float32).reshape(D // TILE, TILE, FF // TILE, TILE)
    scaled = tile_grid * scales.astype(jnp.float32)[:, None, :, None]
    return scaled.reshape(D, FF).astype(jnp.bfloat16)


def reference(primary_q, primary_scales, new_place, tokens, experts, replica, route_num):
    device_count = N_GROUP * N_DEV
    pairs_dev = ROWS_DEV * TOPK
    expert_flat = experts.reshape(-1).astype(jnp.int32)
    pair_total = expert_flat.shape[0]
    holder = jnp.full((EXPERTS,), -1, jnp.int32).at[new_place].set(jnp.arange(device_count, dtype=jnp.int32))
    holder_of = holder[expert_flat]
    use_copy = (replica.reshape(-1) == 1) & (holder_of >= 0)
    target = jnp.where(use_copy, holder_of, expert_flat // EXP_DEV).astype(jnp.int32)
    slot_id = jnp.where(use_copy, EXP_DEV, expert_flat % EXP_DEV).astype(jnp.int32)
    grouped = target.reshape(device_count, pairs_dev)
    is_earlier = jnp.arange(pairs_dev)[None, :] < jnp.arange(pairs_dev)[:, None]
    same_dest = grouped[:, :, None] == grouped[:, None, :]
    position = jnp.sum(same_dest & is_earlier[None], axis=2).astype(jnp.int32).reshape(-1)
    served = position < CAP
    source_dev = (jnp.arange(pair_total, dtype=jnp.int32) // pairs_dev).astype(jnp.int32)
    cell_count = device_count * CAP
    flat_index = (target * cell_count + source_dev * CAP + position).astype(jnp.int32)
    dump_cell = device_count * cell_count
    cell_table = jnp.full((dump_cell + 1,), -1, jnp.int32)
    cell_table = cell_table.at[jnp.where(served, flat_index, dump_cell)].set(jnp.arange(pair_total, dtype=jnp.int32))
    cell_table = cell_table[:dump_cell].reshape(device_count, cell_count)

    def serve_rows(operands):
        device, pair_ids = operands
        is_valid = pair_ids >= 0
        safe_ids = jnp.maximum(pair_ids, 0)
        row_block = jnp.where(is_valid[:, None], tokens[safe_ids // TOPK], jnp.zeros((), tokens.dtype))
        slot_code = jnp.where(is_valid, slot_id[safe_ids], -1)
        matrices = [dequantize(primary_q[device * EXP_DEV + member], primary_scales[device * EXP_DEV + member]) for member in range(EXP_DEV)]
        matrices.append(dequantize(primary_q[new_place[device]], primary_scales[new_place[device]]))
        joined = jnp.concatenate(matrices, axis=1)
        product = jnp.dot(row_block, joined, preferred_element_type=jnp.float32)
        picked = jnp.zeros_like(product[:, :FF])
        for member in range(EXP_DEV + 1):
            picked = picked + jnp.where((slot_code == member)[:, None], product[:, member * FF:(member + 1) * FF], jnp.zeros_like(picked))
        return jax.nn.silu(picked).astype(jnp.bfloat16)

    results = lax.map(serve_rows, (jnp.arange(device_count, dtype=jnp.int32), cell_table))
    gathered = results.reshape(device_count * cell_count, FF)[jnp.where(served, flat_index, 0)]
    selected = jnp.where(served[:, None], gathered.astype(jnp.float32), jnp.zeros((), jnp.float32))
    weight = route_num.reshape(-1).astype(jnp.float32) / 16.0
    hidden_out = (selected * weight[:, None]).astype(jnp.bfloat16).reshape(experts.shape[0], TOPK, FF)
    load_table = jnp.zeros((device_count * (EXP_DEV + 1),), jnp.int32)
    load_table = load_table.at[target * (EXP_DEV + 1) + slot_id].add(served.astype(jnp.int32))
    load_table = load_table.reshape(device_count, EXP_DEV + 1)
    return primary_q[new_place], primary_scales[new_place], hidden_out, load_table
```

```python
import jax
import jax.numpy as jnp
from jax import lax
from jax.experimental import pallas as pl
from jax.experimental.pallas import tpu as pltpu
from jax.sharding import PartitionSpec as P

D = 3584
FF = 1024
TILE = 128
CAP = 2
HOLD = 2
NG = 8
ND = 16
N = NG * ND
ROWS = 16
TOPK = 8
PAIRS = ROWS * TOPK
CELLS = N * CAP
KT = D // TILE
WIDE = D + 128
BF = jnp.bfloat16
F32 = jnp.float32
I32 = jnp.int32
MESH = pl.DeviceIdType.MESH

ORDER = (
    (0, 1), (0, 3), (1, 0), (3, 0), (1, 1), (3, 3), (1, 3), (3, 1),
    (0, 2), (2, 0), (2, 2), (1, 2), (3, 2), (2, 1), (2, 3),
)
CHUNKS = ((2048, 96), (0, 128))
SUB = 16
QROWS = 512


def iota(shape, dim):
    return lax.broadcasted_iota(I32, shape, dim)


def unpack_rows(flat, blocks):
    @pl.loop(0, CELLS // 8)
    def _(i):
        v = flat[pl.ds(pl.multiple_of(8 * i, 8), 8), :]
        for j in range(4):
            blocks[4 * i + j] = v[2 * j : 2 * j + 2].astype(BF)


def pack_rows(blocks, flat):
    @pl.loop(0, CELLS // 8)
    def _(i):
        v = [blocks[4 * i + j].astype(F32) for j in range(4)]
        flat[pl.ds(pl.multiple_of(8 * i, 8), 8), :] = jnp.concatenate(v, axis=0)


def kernel(
    q, scales, place, tokens, experts, replica, route,
    w_out, scale_out, hidden_out, load_out,
    place_tx, place_rx, place_sm, meta_tx, meta_rx,
    relay_a, relay_b, send_a, send_b, w_new,
    big, tx, rx, xm, acc, back_tx, back_rx, qbuf, grow, placed_t,
    sem_place, sem_meta, sem_p1s, sem_p1r, sem_p2s, sem_p2r,
    sem_tok, sem_ret, sem_local, sem_q, sem_w,
):
    g = lax.axis_index("group")
    d = lax.axis_index("dev")
    z, x = d // 4, d % 4
    me = g * ND + d

    def peer(o):
        return lax.rem(z + o[0], 4) * 4 + lax.rem(x + o[1], 4)

    def everyone(off):
        t = lax.rem(me + off, N)
        return t, (t // ND, lax.rem(t, ND))

    def remote(src, dst, ssem, rsem, dev):
        return pltpu.make_async_remote_copy(
            src_ref=src, dst_ref=dst, send_sem=ssem, recv_sem=rsem,
            device_id=dev, device_id_type=MESH,
        )

    place_tx[...] = jnp.full((1, 128), place[0], I32)
    place_rx[me] = jnp.full((1, 128), place[0], I32)
    spread = jnp.zeros((KT, 128), F32)
    for m in range(HOLD):
        pick = (iota((8, 128), 1) == iota((8, 128), 0) + 8 * m).astype(BF)
        spread += jnp.dot(scales[m], pick, preferred_element_type=F32)
    meta_tx[0:KT] = spread.astype(BF)
    meta_tx[KT:] = jnp.zeros((32 - KT, 128), BF)

    barrier = pltpu.get_barrier_semaphore()

    @pl.loop(1, N)
    def _(off):
        _, dev = everyone(off)
        pl.semaphore_signal(barrier, inc=1, device_id=dev, device_id_type=MESH)

    pl.semaphore_wait(barrier, N - 1)

    @pl.loop(1, N)
    def _(off):
        _, dev = everyone(off)
        remote(place_tx, place_rx.at[me], sem_place.at[0], sem_place.at[1], dev).start()

    for o in ORDER:
        remote(meta_tx, meta_rx.at[d], sem_meta.at[0], sem_meta.at[1], (g, peer(o))).start()
    meta_own = pltpu.make_async_copy(meta_tx, meta_rx.at[d], sem_local.at[0])
    meta_own.start()

    relays = (relay_a, relay_b)
    sends = (send_a, send_b)
    own = []
    for c, (base, rows) in enumerate(CHUNKS):
        @pl.loop(0, rows // SUB)
        def _(s, c=c, base=base, rows=rows):
            for o in ORDER:
                p = peer(o)
                remote(
                    q.at[:, pl.ds(pl.multiple_of(base + p * rows + s * SUB, SUB), SUB)],
                    relays[c].at[d, :, pl.ds(pl.multiple_of(s * SUB, SUB), SUB)],
                    sem_p1s.at[c], sem_p1r.at[c], (g, p),
                ).start()
        cp = pltpu.make_async_copy(
            q.at[:, pl.ds(pl.multiple_of(base + d * rows, SUB), rows)], relays[c].at[d], sem_local.at[1 + c]
        )
        cp.start()
        own.append(cp)

    def q_copy(i):
        return pltpu.make_async_copy(
            q.at[i // (D // QROWS), pl.ds(pl.multiple_of(lax.rem(i, D // QROWS) * QROWS, QROWS), QROWS)],
            qbuf.at[lax.rem(i, 2)], sem_q.at[lax.rem(i, 2)],
        )

    q_copy(0).start()

    def to_row(a):
        rep = (lax.rem(iota((TOPK, PAIRS), 1), TOPK) == iota((TOPK, PAIRS), 0)).astype(BF)
        wide = jnp.dot(a[...].astype(F32).astype(BF), rep, preferred_element_type=F32)
        mine = iota((ROWS, PAIRS), 1) // TOPK == iota((ROWS, PAIRS), 0)
        return jnp.sum(jnp.where(mine, wide, 0.0), axis=0, keepdims=True)

    def to_col(row):
        return jnp.broadcast_to(row, (PAIRS, PAIRS)).T

    expert_row = to_row(experts)
    replica_row = to_row(replica)
    weight_col = to_col(to_row(route) * (1.0 / 16.0))

    def wait_recv_all(ref, sem):
        pltpu.make_async_copy(ref, ref, sem).wait()

    wait_recv_all(place_rx.at[pl.ds(0, N - 1)], sem_place.at[1])
    sm = pltpu.make_async_copy(place_rx.at[pl.ds(pl.multiple_of(g * ND, ND), ND)], place_sm, sem_local.at[3])
    sm.start()

    hold_of = place_rx[...].reshape(N, 128).astype(F32)
    match = hold_of == expert_row
    dev_ids = iota((N, PAIRS), 0).astype(F32)
    holder = jnp.sum(jnp.where(match, dev_ids, 0.0), axis=0, keepdims=True)
    found = jnp.sum(jnp.where(match, 1.0, 0.0), axis=0, keepdims=True)
    use_copy = (replica_row > 0.5) & (found > 0.5)
    home = jnp.floor(expert_row * 0.5)
    target = jnp.where(use_copy, holder, home)
    slot = jnp.where(use_copy, float(HOLD), expert_row - 2.0 * home)
    target_col = to_col(target)
    slot_col = to_col(slot)
    earlier = (target_col == target) & (iota((PAIRS, PAIRS), 0) < iota((PAIRS, PAIRS), 1))
    position = jnp.sum(jnp.where(earlier, 1.0, 0.0), axis=0, keepdims=True)
    cell = jnp.where(position < CAP, target * CAP + position, -1.0)
    placed = jnp.where(iota((CELLS, PAIRS), 0).astype(F32) == cell, 1.0, 0.0)
    cell_col = jnp.concatenate([to_col(cell)] * 2, axis=1)
    placed_t[...] = jnp.where(iota((PAIRS, CELLS), 1).astype(F32) == cell_col, 1.0, 0.0).astype(BF)
    placed = placed.astype(BF)
    to_rows = (iota((PAIRS, ROWS), 0) // TOPK == iota((PAIRS, ROWS), 1)).astype(BF)
    row_pick = jnp.dot(placed, to_rows, preferred_element_type=F32).astype(BF)

    @pl.loop(0, D // 512)
    def _(i):
        cols = pl.ds(pl.multiple_of(i * 512, 512), 512)
        big[:, cols] = jnp.dot(row_pick, tokens[:, cols], preferred_element_type=F32)

    big[:, D:] = jnp.dot(placed, (slot_col + 1.0).astype(BF), preferred_element_type=F32) - 1.0

    unpack_rows(big, tx)

    @pl.loop(1, N)
    def _(off):
        t, dev = everyone(off)
        remote(tx.at[t], rx.at[me], sem_tok.at[0], sem_tok.at[1], dev).start()

    tok_own = pltpu.make_async_copy(tx.at[me], rx.at[me], sem_local.at[4])
    tok_own.start()

    sm.wait()

    def relay_select(c):
        base, rows = CHUNKS[c]
        own[c].wait()
        wait_recv_all(relays[c].at[pl.ds(0, ND - 1)], sem_p1r.at[c])

        @pl.loop(0, ND)
        def _(p):
            w = place_sm[p, 0, 0]
            sends[c][p] = relays[c][lax.rem(w // HOLD, ND), lax.rem(w, HOLD)]

        mine = pl.ds(pl.multiple_of(base + d * rows, SUB), rows)
        for i, o in enumerate(ORDER):
            p = peer(o)
            remote(sends[c].at[p], w_new.at[mine], sem_p2s.at[c], sem_p2r.at[i, c], (g, p)).start()
        pltpu.make_async_copy(sends[c].at[d], w_new.at[mine], sem_local.at[5 + c]).start()

    relay_select(0)
    relay_select(1)

    meta_own.wait()
    wait_recv_all(meta_rx.at[pl.ds(0, ND - 1)], sem_meta.at[1])
    mine_w = place[0]
    got = meta_rx[lax.rem(mine_w // HOLD, ND)]
    slot_m = lax.rem(mine_w, HOLD)
    keep = (iota((128, 128), 0) == iota((128, 128), 1) + 8 * slot_m).astype(BF)
    scale_out[...] = jnp.dot(got, keep, preferred_element_type=F32).astype(BF)

    def grow_scales(block, m):
        sel = (iota((128, FF), 0) == iota((128, FF), 1) // TILE + 8 * m).astype(BF)
        return jnp.dot(block, sel, preferred_element_type=F32).reshape(32, 1, FF)

    for m in range(HOLD):
        grow[m] = grow_scales(meta_tx[...], m)
    grow[HOLD] = grow_scales(got, slot_m)

    tok_own.wait()
    wait_recv_all(rx.at[pl.ds(0, N - 1)], sem_tok.at[1])

    pack_rows(rx, big)

    code = big[:, D:]
    load_row = jnp.zeros((1, 128), F32)
    for s in range(HOLD + 1):
        count = jnp.sum(jnp.where(code == float(s), 1.0, 0.0), axis=0, keepdims=True)
        load_row = jnp.where(iota((1, 128), 1) == s, count, load_row)
    load_out[...] = jnp.broadcast_to(load_row, (8, 128)).astype(I32)

    for s in range(HOLD + 1):
        @pl.loop(0, KT)
        def _(k, s=s):
            cols = pl.ds(pl.multiple_of(k * TILE, TILE), TILE)
            xm[s, :, cols] = jnp.where(code == float(s), big[:, cols], 0.0).astype(BF)

    acc[...] = jnp.zeros((CELLS, FF), F32)
    n_q = HOLD * (D // QROWS)

    @pl.loop(0, n_q)
    def _(i):
        @pl.when(i + 1 < n_q)
        def _():
            q_copy(i + 1).start()
        q_copy(i).wait()
        m = i // (D // QROWS)
        tile0 = lax.rem(i, D // QROWS) * (QROWS // TILE)
        w = qbuf[lax.rem(i, 2)].astype(F32).reshape(QROWS // TILE, TILE, FF)
        w = (w * grow[m, pl.ds(tile0, QROWS // TILE)]).astype(BF).reshape(QROWS, FF)
        xs = xm[m, :, pl.ds(pl.multiple_of(tile0 * TILE, TILE), QROWS)]
        acc[...] += jnp.dot(xs, w, preferred_element_type=F32)

    def w_tile(k, n):
        rows = pl.ds(pl.multiple_of(k * TILE, TILE), n * TILE)
        w = w_new[rows].astype(F32).reshape(n, TILE, FF)
        w = (w * grow[HOLD, pl.ds(k, n)]).astype(BF).reshape(n * TILE, FF)
        acc[...] += jnp.dot(xm[HOLD, :, rows], w, preferred_element_type=F32)

    def w_wait(i, c):
        base, rows = CHUNKS[c]
        ref = w_new.at[pl.ds(base, rows)]
        pltpu.make_async_copy(ref, ref, sem_p2r.at[i, c]).wait()

    def w_own(c):
        base, rows = CHUNKS[c]
        mine = pl.ds(pl.multiple_of(base + d * rows, SUB), rows)
        pltpu.make_async_copy(sends[c].at[d], w_new.at[mine], sem_local.at[5 + c]).wait()

    w_own(0)
    for i in range(len(ORDER)):
        w_wait(i, 0)
    out_a = pltpu.make_async_copy(w_new.at[pl.ds(2048, 1536)], w_out.at[pl.ds(2048, 1536)], sem_w.at[0])
    out_a.start()

    @pl.loop(0, 3)
    def _(i):
        w_tile(16 + 4 * i, 4)

    w_own(1)
    w_tile(d, 1)
    for i, o in enumerate(ORDER):
        w_wait(i, 1)
        k = lax.rem(z + 4 - o[0], 4) * 4 + lax.rem(x + 4 - o[1], 4)
        w_tile(k, 1)
    out_b = pltpu.make_async_copy(w_new.at[pl.ds(0, 2048)], w_out.at[pl.ds(0, 2048)], sem_w.at[1])
    out_b.start()

    v = acc[...]
    acc[...] = v / (1.0 + jnp.exp(-v))

    unpack_rows(acc, back_tx)

    @pl.loop(1, N)
    def _(off):
        t, dev = everyone(off)
        remote(back_tx.at[t], back_rx.at[me], sem_ret.at[0], sem_ret.at[1], dev).start()

    ret_own = pltpu.make_async_copy(back_tx.at[me], back_rx.at[me], sem_local.at[7])
    ret_own.start()
    ret_own.wait()
    wait_recv_all(back_rx.at[pl.ds(0, N - 1)], sem_ret.at[1])

    pack_rows(back_rx, acc)

    selected = jnp.dot(placed_t[...], acc[...].astype(BF), preferred_element_type=F32)
    hidden_out[...] = (selected * weight_col[:, 0:1]).astype(BF)

    wait_recv_all(place_rx.at[pl.ds(0, N - 1)], sem_place.at[0])
    wait_recv_all(meta_rx.at[pl.ds(0, ND - 1)], sem_meta.at[0])
    for c in range(2):
        wait_recv_all(relays[c].at[pl.ds(0, ND - 1)], sem_p1s.at[c])
        wait_recv_all(sends[c].at[pl.ds(0, ND - 1)], sem_p2s.at[c])
    wait_recv_all(tx.at[pl.ds(0, N - 1)], sem_tok.at[0])
    wait_recv_all(back_tx.at[pl.ds(0, N - 1)], sem_ret.at[0])
    out_a.wait()
    out_b.wait()


def per_device(primary_q, primary_scales, new_place, tokens, experts, replica, route_num):
    vmem = pl.BlockSpec(memory_space=pltpu.VMEM)
    anywhere = pl.BlockSpec(memory_space=pl.ANY)
    dma = pltpu.SemaphoreType.DMA
    scratch = [
        pltpu.VMEM((1, 128), I32),
        pltpu.VMEM((N, 1, 128), I32),
        pltpu.SMEM((ND, 1, 128), I32),
        pltpu.VMEM((32, 128), BF),
        pltpu.VMEM((ND, 32, 128), BF),
        pltpu.VMEM((ND, HOLD, CHUNKS[0][1], FF), BF),
        pltpu.VMEM((ND, HOLD, CHUNKS[1][1], FF), BF),
        pltpu.VMEM((ND, CHUNKS[0][1], FF), BF),
        pltpu.VMEM((ND, CHUNKS[1][1], FF), BF),
        pltpu.VMEM((D, FF), BF),
        pltpu.VMEM((CELLS, WIDE), F32),
        pltpu.VMEM((N, CAP, WIDE), BF),
        pltpu.VMEM((N, CAP, WIDE), BF),
        pltpu.VMEM((HOLD + 1, CELLS, D), BF),
        pltpu.VMEM((CELLS, FF), F32),
        pltpu.VMEM((N, CAP, FF), BF),
        pltpu.VMEM((N, CAP, FF), BF),
        pltpu.VMEM((2, QROWS, FF), BF),
        pltpu.VMEM((HOLD + 1, 32, 1, FF), F32),
        pltpu.VMEM((PAIRS, CELLS), BF),
        dma((2,)), dma((2,)), dma((2,)), dma((2,)), dma((2,)), dma((len(ORDER), 2)),
        dma((2,)), dma((2,)), dma((8,)), dma((2,)), dma((2,)),
    ]
    new_weights, scale_tile, hidden, load = pl.pallas_call(
        kernel,
        out_shape=(
            jax.ShapeDtypeStruct((D, FF), BF),
            jax.ShapeDtypeStruct((32, 128), BF),
            jax.ShapeDtypeStruct((PAIRS, FF), BF),
            jax.ShapeDtypeStruct((8, 128), I32),
        ),
        in_specs=[
            anywhere, vmem, pl.BlockSpec(memory_space=pltpu.SMEM), vmem, vmem, vmem, vmem,
        ],
        out_specs=(anywhere, vmem, vmem, vmem),
        scratch_shapes=scratch,
        compiler_params=pltpu.CompilerParams(
            collective_id=0, has_side_effects=True, vmem_limit_bytes=64000 * 1024
        ),
    )(primary_q, primary_scales, new_place, tokens, experts, replica, route_num)
    return (
        new_weights.reshape(1, D, FF),
        scale_tile[:KT, :8].reshape(1, KT, 8),
        hidden.reshape(ROWS, TOPK, FF),
        load[0:1, : HOLD + 1],
    )


def solution(mesh):
    both = ("group", "dev")
    return jax.shard_map(
        per_device,
        mesh=mesh,
        in_specs=(
            P(both, None, None), P(both, None, None), P(both), P(both, None),
            P(both, None), P(both, None), P(both, None),
        ),
        out_specs=(P(both, None, None), P(both, None, None), P(both, None, None), P(both, None)),
        check_vma=False,
    )
```

```python
import jax
import jax.numpy as jnp
from jax import lax
from jax.experimental import pallas as pl
from jax.experimental.pallas import tpu as pltpu
from jax.sharding import PartitionSpec as P

D = 3584
FF = 1024
TILE = 128
CAP = 2
HOLD = 2
NG = 8
ND = 16
N = NG * ND
ROWS = 16
TOPK = 8
PAIRS = ROWS * TOPK
CELLS = N * CAP
KT = D // TILE
WIDE = D + 128
BF = jnp.bfloat16
F32 = jnp.float32
I32 = jnp.int32
MESH = pl.DeviceIdType.MESH

ORDER = (
    (0, 1), (0, 3), (1, 0), (3, 0), (1, 1), (3, 3), (1, 3), (3, 1),
    (0, 2), (2, 0), (2, 2), (1, 2), (3, 2), (2, 1), (2, 3),
)
CHUNKS = ((2048, 96), (0, 128))
SUB = 16
EARLY = 3
QROWS = 512


def iota(shape, dim):
    return lax.broadcasted_iota(I32, shape, dim)


def unpack_rows(flat, blocks):
    @pl.loop(0, CELLS // 8)
    def _(i):
        v = flat[pl.ds(pl.multiple_of(8 * i, 8), 8), :]
        for j in range(4):
            blocks[4 * i + j] = v[2 * j : 2 * j + 2].astype(BF)


def pack_rows(blocks, flat, nested=False):
    @pl.loop(0, CELLS // 8)
    def _(i):
        at = [(i // 2, lax.rem(i, 2) * 4 + j) if nested else (4 * i + j,) for j in range(4)]
        v = [blocks[a].astype(F32) for a in at]
        flat[pl.ds(pl.multiple_of(8 * i, 8), 8), :] = jnp.concatenate(v, axis=0)


def kernel(
    q, scales, place, tokens, experts, replica, route,
    w_out, scale_out, hidden_out, load_out,
    place_tx, place_rx, place_sm, meta_tx, meta_rx,
    relay_a, relay_b, send_a, send_b, w_new,
    big, tx, mid, rx, xm, acc, back_tx, back_mid, back_rx, qbuf, grow, placed_t,
    sem_place, sem_spread, sem_meta, sem_p1s, sem_p1r, sem_p2s, sem_p2r,
    sem_tok, sem_tok2, sem_ret, sem_ret2, sem_local, sem_q, sem_w,
):
    g = lax.axis_index("group")
    d = lax.axis_index("dev")
    z, x = d // 4, d % 4
    me = g * ND + d

    def peer(o):
        return lax.rem(z + o[0], 4) * 4 + lax.rem(x + o[1], 4)

    def remote(src, dst, ssem, rsem, dev):
        return pltpu.make_async_remote_copy(
            src_ref=src, dst_ref=dst, send_sem=ssem, recv_sem=rsem,
            device_id=dev, device_id_type=MESH,
        )

    def across(i):
        return lax.rem(g + i, NG)

    place_tx[...] = jnp.full((1, 128), place[0], I32)
    place_rx[me] = jnp.full((1, 128), place[0], I32)
    widen = (iota((KT, 128), 0) == iota((KT, 128), 1)).astype(BF)
    spread = [jnp.dot(scales[m], widen, preferred_element_type=F32) for m in range(HOLD)]
    meta_tx[...] = jnp.concatenate(spread, axis=0).astype(BF)

    barrier = pltpu.get_barrier_semaphore()

    for o in ORDER:
        pl.semaphore_signal(barrier, inc=1, device_id=(g, peer(o)), device_id_type=MESH)
    for i in range(1, NG):
        pl.semaphore_signal(barrier, inc=1, device_id=(across(i), d), device_id_type=MESH)
    pl.semaphore_wait(barrier, ND - 1 + NG - 1)

    for o in ORDER:
        remote(place_tx, place_rx.at[me], sem_place.at[0], sem_place.at[1], (g, peer(o))).start()
    for o in ORDER:
        remote(meta_tx, meta_rx.at[d], sem_meta.at[0], sem_meta.at[1], (g, peer(o))).start()
    meta_own = pltpu.make_async_copy(meta_tx, meta_rx.at[d], sem_local.at[0])
    meta_own.start()

    relays = (relay_a, relay_b)
    sends = (send_a, send_b)
    own = []

    def spread_rows(c, lo, hi):
        base, rows = CHUNKS[c]

        @pl.loop(lo, hi)
        def _(s):
            for o in ORDER:
                p = peer(o)
                remote(
                    q.at[:, pl.ds(pl.multiple_of(base + p * rows + s * SUB, SUB), SUB)],
                    relays[c].at[d, :, pl.ds(pl.multiple_of(s * SUB, SUB), SUB)],
                    sem_p1s.at[c], sem_p1r.at[c], (g, p),
                ).start()

    spread_rows(0, 0, EARLY)
    for c, (base, rows) in enumerate(CHUNKS):
        cp = pltpu.make_async_copy(
            q.at[:, pl.ds(pl.multiple_of(base + d * rows, SUB), rows)], relays[c].at[d], sem_local.at[1 + c]
        )
        cp.start()
        own.append(cp)

    def q_copy(i):
        return pltpu.make_async_copy(
            q.at[i // (D // QROWS), pl.ds(pl.multiple_of(lax.rem(i, D // QROWS) * QROWS, QROWS), QROWS)],
            qbuf.at[lax.rem(i, 2)], sem_q.at[lax.rem(i, 2)],
        )

    q_copy(0).start()

    def to_row(a):
        rep = (iota((ROWS, PAIRS), 1) // TOPK == iota((ROWS, PAIRS), 0)).astype(BF)
        wide = jnp.dot(a[...].astype(F32).astype(BF), rep, preferred_element_type=F32)
        mine = lax.rem(iota((TOPK, PAIRS), 1), TOPK) == iota((TOPK, PAIRS), 0)
        return jnp.sum(jnp.where(mine, wide, 0.0), axis=0, keepdims=True)

    def to_col(row):
        return jnp.broadcast_to(row, (PAIRS, PAIRS)).T

    expert_row = to_row(experts)
    replica_row = to_row(replica)
    weight_col = to_col(to_row(route) * (1.0 / 16.0))

    def wait_recv_all(ref, sem):
        pltpu.make_async_copy(ref, ref, sem).wait()

    group_rows = pl.ds(pl.multiple_of(g * ND, ND), ND)
    wait_recv_all(place_rx.at[pl.ds(0, ND - 1)], sem_place.at[1])
    for i in range(1, NG):
        remote(
            place_rx.at[group_rows], place_rx.at[group_rows], sem_spread.at[0], sem_spread.at[1], (across(i), d)
        ).start()
    sm = pltpu.make_async_copy(place_rx.at[group_rows], place_sm, sem_local.at[3])
    sm.start()
    wait_recv_all(place_rx.at[pl.ds(0, ND * (NG - 1))], sem_spread.at[1])

    hold_of = place_rx[...].reshape(N, 128).astype(F32)
    match = hold_of == expert_row
    dev_ids = iota((N, PAIRS), 0).astype(F32)
    holder = jnp.sum(jnp.where(match, dev_ids, 0.0), axis=0, keepdims=True)
    found = jnp.sum(jnp.where(match, 1.0, 0.0), axis=0, keepdims=True)
    use_copy = (replica_row > 0.5) & (found > 0.5)
    home = jnp.floor(expert_row * 0.5)
    target = jnp.where(use_copy, holder, home)
    slot = jnp.where(use_copy, float(HOLD), expert_row - 2.0 * home)
    target_col = to_col(target)
    slot_col = to_col(slot)
    earlier = (target_col == target) & (iota((PAIRS, PAIRS), 0) < iota((PAIRS, PAIRS), 1))
    position = jnp.sum(jnp.where(earlier, 1.0, 0.0), axis=0, keepdims=True)
    cell = jnp.where(position < CAP, target * CAP + position, -1.0)
    placed = jnp.where(iota((CELLS, PAIRS), 0).astype(F32) == cell, 1.0, 0.0)
    cell_col = jnp.concatenate([to_col(cell)] * 2, axis=1)
    placed_t[...] = jnp.where(iota((PAIRS, CELLS), 1).astype(F32) == cell_col, 1.0, 0.0).astype(BF)
    placed = placed.astype(BF)
    to_rows = (iota((PAIRS, ROWS), 0) // TOPK == iota((PAIRS, ROWS), 1)).astype(BF)
    row_pick = jnp.dot(placed, to_rows, preferred_element_type=F32).astype(BF)

    @pl.loop(0, D // 512)
    def _(i):
        cols = pl.ds(pl.multiple_of(i * 512, 512), 512)
        big[:, cols] = jnp.dot(row_pick, tokens[:, cols], preferred_element_type=F32)

    big[:, D:] = jnp.dot(placed, (slot_col + 1.0).astype(BF), preferred_element_type=F32) - 1.0

    unpack_rows(big, tx)

    for i in range(1, NG):
        t = across(i)
        remote(
            tx.at[pl.ds(pl.multiple_of(t * ND, ND), ND)], mid.at[g], sem_tok.at[0], sem_tok.at[1], (t, d)
        ).start()
    mid_own = pltpu.make_async_copy(tx.at[group_rows], mid.at[g], sem_local.at[8])
    mid_own.start()
    spread_rows(0, EARLY, CHUNKS[0][1] // SUB)
    mid_own.wait()
    wait_recv_all(mid.at[pl.ds(0, NG - 1)], sem_tok.at[1])
    for o in ORDER:
        p = peer(o)
        remote(mid.at[:, p], rx.at[d], sem_tok2.at[0], sem_tok2.at[1], (g, p)).start()
    tok_own = pltpu.make_async_copy(mid.at[:, d], rx.at[d], sem_local.at[4])
    tok_own.start()
    spread_rows(1, 0, CHUNKS[1][1] // SUB)


    sm.wait()

    def relay_select(c):
        base, rows = CHUNKS[c]
        own[c].wait()
        wait_recv_all(relays[c].at[pl.ds(0, ND - 1)], sem_p1r.at[c])

        @pl.loop(0, ND)
        def _(p):
            w = place_sm[p, 0, 0]
            sends[c][p] = relays[c][lax.rem(w // HOLD, ND), lax.rem(w, HOLD)]

        mine = pl.ds(pl.multiple_of(base + d * rows, SUB), rows)
        for i, o in enumerate(ORDER):
            p = peer(o)
            remote(sends[c].at[p], w_new.at[mine], sem_p2s.at[c], sem_p2r.at[i, c], (g, p)).start()
        pltpu.make_async_copy(sends[c].at[d], w_new.at[mine], sem_local.at[5 + c]).start()

    relay_select(0)
    relay_select(1)

    meta_own.wait()
    wait_recv_all(meta_rx.at[pl.ds(0, ND - 1)], sem_meta.at[1])
    mine_w = place[0]
    got = meta_rx[lax.rem(mine_w // HOLD, ND)]
    slot_m = lax.rem(mine_w, HOLD)
    got_wide = got.astype(F32)
    mine_scales = jnp.where(slot_m == 0, got_wide[0:8], got_wide[8:16])
    scale_out[...] = mine_scales[:, 0:KT].astype(BF)

    def grow_scales(block, m):
        sel = (iota((128, FF), 0) == iota((128, FF), 1) // TILE + 8 * m).astype(BF)
        tall = jnp.concatenate([block.astype(F32), jnp.zeros((112, 128), F32)], axis=0).T
        return jnp.dot(tall[0:32].astype(BF), sel, preferred_element_type=F32).reshape(32, 1, FF)

    for m in range(HOLD):
        grow[m] = grow_scales(meta_tx[...], m)
    grow[HOLD] = grow_scales(got, slot_m)

    tok_own.wait()
    wait_recv_all(rx.at[pl.ds(0, ND - 1)], sem_tok2.at[1])

    pack_rows(rx, big, True)

    code = big[:, D:]
    load_row = jnp.zeros((1, 128), F32)
    for s in range(HOLD + 1):
        count = jnp.sum(jnp.where(code == float(s), 1.0, 0.0), axis=0, keepdims=True)
        load_row = jnp.where(iota((1, 128), 1) == s, count, load_row)
    load_out[...] = load_row[:, 0 : HOLD + 1].astype(I32)

    for s in range(HOLD + 1):
        @pl.loop(0, KT)
        def _(k, s=s):
            cols = pl.ds(pl.multiple_of(k * TILE, TILE), TILE)
            xm[s, :, cols] = jnp.where(code == float(s), big[:, cols], 0.0).astype(BF)

    acc[...] = jnp.zeros((CELLS, FF), F32)
    n_q = HOLD * (D // QROWS)

    @pl.loop(0, n_q)
    def _(i):
        @pl.when(i + 1 < n_q)
        def _():
            q_copy(i + 1).start()
        q_copy(i).wait()
        m = i // (D // QROWS)
        tile0 = lax.rem(i, D // QROWS) * (QROWS // TILE)
        w = qbuf[lax.rem(i, 2)].astype(F32).reshape(QROWS // TILE, TILE, FF)
        w = (w * grow[m, pl.ds(tile0, QROWS // TILE)]).astype(BF).reshape(QROWS, FF)
        xs = xm[m, :, pl.ds(pl.multiple_of(tile0 * TILE, TILE), QROWS)]
        acc[...] += jnp.dot(xs, w, preferred_element_type=F32)

    def w_tile(k, n):
        rows = pl.ds(pl.multiple_of(k * TILE, TILE), n * TILE)
        w = w_new[rows].astype(F32).reshape(n, TILE, FF)
        w = (w * grow[HOLD, pl.ds(k, n)]).astype(BF).reshape(n * TILE, FF)
        acc[...] += jnp.dot(xm[HOLD, :, rows], w, preferred_element_type=F32)

    def w_wait(i, c):
        base, rows = CHUNKS[c]
        ref = w_new.at[pl.ds(base, rows)]
        pltpu.make_async_copy(ref, ref, sem_p2r.at[i, c]).wait()

    def w_own(c):
        base, rows = CHUNKS[c]
        mine = pl.ds(pl.multiple_of(base + d * rows, SUB), rows)
        pltpu.make_async_copy(sends[c].at[d], w_new.at[mine], sem_local.at[5 + c]).wait()

    w_own(0)
    for i in range(len(ORDER)):
        w_wait(i, 0)
    out_a = pltpu.make_async_copy(w_new.at[pl.ds(2048, 1536)], w_out.at[pl.ds(2048, 1536)], sem_w.at[0])
    out_a.start()

    @pl.loop(0, 3)
    def _(i):
        w_tile(16 + 4 * i, 4)

    w_own(1)
    w_tile(d, 1)
    for i, o in enumerate(ORDER):
        w_wait(i, 1)
        k = lax.rem(z + 4 - o[0], 4) * 4 + lax.rem(x + 4 - o[1], 4)
        w_tile(k, 1)
    out_b = pltpu.make_async_copy(w_new.at[pl.ds(0, 2048)], w_out.at[pl.ds(0, 2048)], sem_w.at[1])
    out_b.start()

    v = acc[...]
    acc[...] = v / (1.0 + jnp.exp(-v))

    unpack_rows(acc, back_tx)

    def back_rows(p):
        return pl.ds(pl.multiple_of(p * NG, NG), NG)

    for o in ORDER:
        p = peer(o)
        remote(back_tx.at[back_rows(p)], back_mid.at[:, d], sem_ret.at[0], sem_ret.at[1], (g, p)).start()
    ret_own = pltpu.make_async_copy(back_tx.at[back_rows(d)], back_mid.at[:, d], sem_local.at[7])
    ret_own.start()
    ret_own.wait()
    wait_recv_all(back_mid.at[:, pl.ds(0, ND - 1)], sem_ret.at[1])
    for i in range(1, NG):
        t = across(i)
        remote(back_mid.at[t], back_rx.at[group_rows], sem_ret2.at[0], sem_ret2.at[1], (t, d)).start()
    back_own = pltpu.make_async_copy(back_mid.at[g], back_rx.at[group_rows], sem_local.at[9])
    back_own.start()
    back_own.wait()
    wait_recv_all(back_rx.at[pl.ds(0, ND * (NG - 1))], sem_ret2.at[1])

    pack_rows(back_rx, acc)

    selected = jnp.dot(placed_t[...], acc[...].astype(BF), preferred_element_type=F32)
    hidden_out[...] = (selected * weight_col[:, 0:1]).astype(BF)

    wait_recv_all(place_rx.at[pl.ds(0, ND - 1)], sem_place.at[0])
    wait_recv_all(place_rx.at[pl.ds(0, ND * (NG - 1))], sem_spread.at[0])
    wait_recv_all(meta_rx.at[pl.ds(0, ND - 1)], sem_meta.at[0])
    for c in range(2):
        wait_recv_all(relays[c].at[pl.ds(0, ND - 1)], sem_p1s.at[c])
        wait_recv_all(sends[c].at[pl.ds(0, ND - 1)], sem_p2s.at[c])
    wait_recv_all(mid.at[pl.ds(0, NG - 1)], sem_tok.at[0])
    wait_recv_all(rx.at[pl.ds(0, ND - 1)], sem_tok2.at[0])
    wait_recv_all(back_mid.at[:, pl.ds(0, ND - 1)], sem_ret.at[0])
    wait_recv_all(back_rx.at[pl.ds(0, ND * (NG - 1))], sem_ret2.at[0])
    out_a.wait()
    out_b.wait()


def per_device(primary_q, primary_scales, new_place, tokens, experts, replica, route_num):
    vmem = pl.BlockSpec(memory_space=pltpu.VMEM)
    anywhere = pl.BlockSpec(memory_space=pl.ANY)
    dma = pltpu.SemaphoreType.DMA
    scratch = [
        pltpu.VMEM((1, 128), I32),
        pltpu.VMEM((N, 1, 128), I32),
        pltpu.SMEM((ND, 1, 128), I32),
        pltpu.VMEM((16, 128), BF),
        pltpu.VMEM((ND, 16, 128), BF),
        pltpu.VMEM((ND, HOLD, CHUNKS[0][1], FF), BF),
        pltpu.VMEM((ND, HOLD, CHUNKS[1][1], FF), BF),
        pltpu.VMEM((ND, CHUNKS[0][1], FF), BF),
        pltpu.VMEM((ND, CHUNKS[1][1], FF), BF),
        pltpu.VMEM((D, FF), BF),
        pltpu.VMEM((CELLS, WIDE), F32),
        pltpu.VMEM((N, CAP, WIDE), BF),
        pltpu.VMEM((NG, ND, CAP, WIDE), BF),
        pltpu.VMEM((ND, NG, CAP, WIDE), BF),
        pltpu.VMEM((HOLD + 1, CELLS, D), BF),
        pltpu.VMEM((CELLS, FF), F32),
        pltpu.VMEM((N, CAP, FF), BF),
        pltpu.VMEM((NG, ND, CAP, FF), BF),
        pltpu.VMEM((N, CAP, FF), BF),
        pltpu.VMEM((2, QROWS, FF), BF),
        pltpu.VMEM((HOLD + 1, 32, 1, FF), F32),
        pltpu.VMEM((PAIRS, CELLS), BF),
        dma((2,)), dma((2,)), dma((2,)), dma((2,)), dma((2,)), dma((2,)), dma((len(ORDER), 2)),
        dma((2,)), dma((2,)), dma((2,)), dma((2,)), dma((10,)), dma((2,)), dma((2,)),
    ]
    new_weights, scale_tile, hidden, load = pl.pallas_call(
        kernel,
        out_shape=(
            jax.ShapeDtypeStruct((D, FF), BF),
            jax.ShapeDtypeStruct((8, KT), BF),
            jax.ShapeDtypeStruct((PAIRS, FF), BF),
            jax.ShapeDtypeStruct((1, HOLD + 1), I32),
        ),
        in_specs=[
            anywhere, vmem, pl.BlockSpec(memory_space=pltpu.SMEM), vmem, vmem, vmem, vmem,
        ],
        out_specs=(anywhere, vmem, vmem, vmem),
        scratch_shapes=scratch,
        compiler_params=pltpu.CompilerParams(
            collective_id=0, has_side_effects=True, vmem_limit_bytes=64000 * 1024
        ),
    )(
        primary_q, primary_scales.transpose(0, 2, 1), new_place, tokens,
        experts.T, replica.T, route_num.T,
    )
    return (
        new_weights.reshape(1, D, FF),
        scale_tile.T.reshape(1, KT, 8),
        hidden.reshape(ROWS, TOPK, FF),
        load,
    )


def solution(mesh):
    both = ("group", "dev")
    return jax.shard_map(
        per_device,
        mesh=mesh,
        in_specs=(
            P(both, None, None), P(both, None, None), P(both), P(both, None),
            P(both, None), P(both, None), P(both, None),
        ),
        out_specs=(P(both, None, None), P(both, None, None), P(both, None, None), P(both, None)),
        check_vma=False,
    )
```

```python
import jax
import jax.numpy as jnp
from jax import lax
from jax.experimental import pallas as pl
from jax.experimental.pallas import tpu as pltpu
from jax.sharding import PartitionSpec as P

D = 3584
FF = 1024
TILE = 128
CAP = 2
HOLD = 2
NG = 8
ND = 16
N = NG * ND
ROWS = 16
TOPK = 8
PAIRS = ROWS * TOPK
CELLS = N * CAP
KT = D // TILE
WIDE = D + 128
BF = jnp.bfloat16
F32 = jnp.float32
I32 = jnp.int32
MESH = pl.DeviceIdType.MESH

ORDER = (
    (0, 1), (0, 3), (1, 0), (3, 0), (1, 1), (3, 3), (1, 3), (3, 1),
    (0, 2), (2, 0), (2, 2), (1, 2), (3, 2), (2, 1), (2, 3),
)
CHUNKS = ((0, 0, 0, 512, 0), (0, 1, 512, 384, 1), (1, 0, 0, 512, 1), (1, 1, 512, 384, 0))
PIECE = 896
HALF = 512
SUB = 128
EARLY = 2
QROWS = 512


def iota(shape, dim):
    return lax.broadcasted_iota(I32, shape, dim)


def unpack_rows(flat, blocks):
    @pl.loop(0, CELLS // 8)
    def _(i):
        v = flat[pl.ds(pl.multiple_of(8 * i, 8), 8), :]
        for j in range(4):
            blocks[4 * i + j] = v[2 * j : 2 * j + 2].astype(BF)


def pack_rows(blocks, flat, nested=False):
    @pl.loop(0, CELLS // 8)
    def _(i):
        at = [(i // 2, lax.rem(i, 2) * 4 + j) if nested else (4 * i + j,) for j in range(4)]
        v = [blocks[a].astype(F32) for a in at]
        flat[pl.ds(pl.multiple_of(8 * i, 8), 8), :] = jnp.concatenate(v, axis=0)


def kernel(
    q, scales, place, tokens, experts, replica, route,
    w_out, scale_out, hidden_out, load_out,
    place_tx, place_rx, place_sm, meta_tx, meta_rx,
    r0, r1, r2, r3, y0, y1, y2, y3, s0, s1, s2, s3, w_new,
    big, tx, mid, rx, xm, acc, back_tx, back_mid, back_rx, qbuf, grow, placed_t,
    sem_place, sem_spread, sem_meta, sem_1s, sem_1r, sem_2s, sem_2r, sem_3s, sem_3r, sem_own1, sem_own3,
    sem_tok, sem_tok2, sem_ret, sem_ret2, sem_local, sem_q, sem_w,
):
    g = lax.axis_index("group")
    d = lax.axis_index("dev")
    z, x = d // 4, d % 4
    me = g * ND + d

    def peer(o):
        return lax.rem(z + o[0], 4) * 4 + lax.rem(x + o[1], 4)

    def remote(src, dst, ssem, rsem, dev):
        return pltpu.make_async_remote_copy(
            src_ref=src, dst_ref=dst, send_sem=ssem, recv_sem=rsem,
            device_id=dev, device_id_type=MESH,
        )

    def across(i):
        return lax.rem(g + i, NG)

    place_tx[...] = jnp.full((1, 128), place[0], I32)
    place_rx[me] = jnp.full((1, 128), place[0], I32)
    widen = (iota((KT, 128), 0) == iota((KT, 128), 1)).astype(BF)
    spread = [jnp.dot(scales[m], widen, preferred_element_type=F32) for m in range(HOLD)]
    meta_tx[...] = jnp.concatenate(spread, axis=0).astype(BF)

    barrier = pltpu.get_barrier_semaphore()

    for o in ORDER:
        pl.semaphore_signal(barrier, inc=1, device_id=(g, peer(o)), device_id_type=MESH)
    for i in range(1, NG):
        pl.semaphore_signal(barrier, inc=1, device_id=(across(i), d), device_id_type=MESH)
    pl.semaphore_wait(barrier, ND - 1 + NG - 1)

    for o in ORDER:
        remote(place_tx, place_rx.at[me], sem_place.at[0], sem_place.at[1], (g, peer(o))).start()
    for o in ORDER:
        remote(meta_tx, meta_rx.at[d], sem_meta.at[0], sem_meta.at[1], (g, peer(o))).start()
    meta_own = pltpu.make_async_copy(meta_tx, meta_rx.at[d], sem_local.at[0])
    meta_own.start()

    relays = (r0, r1, r2, r3)
    swaps = (y0, y1, y2, y3)
    sends = (s0, s1, s2, s3)

    def place_of(axis):
        return (z, x) if axis == 0 else (x, z)

    def dev_of(axis, u, v):
        return u * 4 + v if axis == 0 else v * 4 + u

    def mod4(i):
        return lax.rem(i + 8, 4)

    def piece_rows(c, first, n):
        return pl.ds(pl.multiple_of(c * PIECE + first, 128), n)

    def piece_cols(r, f):
        return pl.ds(pl.multiple_of(r * 256 + f * 128, 128), 128)

    KINDS = ((0, 0, 0, 1), (0, 1, -1, 0), (1, 0, 1, 0), (-1, 1, -2, 1))
    FIRST = ((1, 0), (3, 0), (0, 2), (0, 3), (1, 1), (3, 1), (1, 2), (3, 3), (3, 2), (1, 3), (2, 0), (2, 2), (2, 1), (2, 3))

    def supply(k, dv, kind, at, n):
        f, _, base, rows, axis = CHUNKS[k]
        u, v = place_of(axis)
        step, role, piece, line = KINDS[kind]
        r = mod4(v + dv)
        src = q.at[:, piece_rows(mod4(u + piece), base + at, n), piece_cols(r, f)]
        entry = role * 16 + (line * 4 + v) * 2
        dst = relays[k].at[pl.ds(entry, 2), pl.ds(pl.multiple_of(at, 128), n)]
        return src, dst, (g, dev_of(axis, mod4(u + step), r))

    def supply_sends(ks, at):
        for dv, kind in FIRST:
            for k in ks:
                src, dst, dev = supply(k, dv, kind, at, SUB)
                remote(src, dst, sem_1s.at[k], sem_1r.at[k], dev).start()

    def supply_own(k):
        cps = []
        for kind in range(2):
            src, dst, _ = supply(k, 0, kind, 0, CHUNKS[k][3])
            cps.append(pltpu.make_async_copy(src, dst, sem_own1.at[k, kind]))
        return cps

    def supply_steps(pair, lo, hi):
        @pl.loop(lo, hi)
        def _(i):
            supply_sends(pair, i * SUB)

    supply_steps((0, 1), 0, EARLY)
    own = [supply_own(k) for k in range(4)]
    for cps in own:
        for cp in cps:
            cp.start()

    def q_copy(i):
        return pltpu.make_async_copy(
            q.at[i // (D // QROWS), pl.ds(pl.multiple_of(lax.rem(i, D // QROWS) * QROWS, QROWS), QROWS)],
            qbuf.at[lax.rem(i, 2)], sem_q.at[lax.rem(i, 2)],
        )

    q_copy(0).start()

    def to_row(a):
        rep = (iota((ROWS, PAIRS), 1) // TOPK == iota((ROWS, PAIRS), 0)).astype(BF)
        wide = jnp.dot(a[...].astype(F32).astype(BF), rep, preferred_element_type=F32)
        mine = lax.rem(iota((TOPK, PAIRS), 1), TOPK) == iota((TOPK, PAIRS), 0)
        return jnp.sum(jnp.where(mine, wide, 0.0), axis=0, keepdims=True)

    def to_col(row):
        return jnp.broadcast_to(row, (PAIRS, PAIRS)).T

    expert_row = to_row(experts)
    replica_row = to_row(replica)
    weight_col = to_col(to_row(route) * (1.0 / 16.0))

    def wait_recv_all(ref, sem):
        pltpu.make_async_copy(ref, ref, sem).wait()

    group_rows = pl.ds(pl.multiple_of(g * ND, ND), ND)
    wait_recv_all(place_rx.at[pl.ds(0, ND - 1)], sem_place.at[1])
    for i in range(1, NG):
        remote(
            place_rx.at[group_rows], place_rx.at[group_rows], sem_spread.at[0], sem_spread.at[1], (across(i), d)
        ).start()
    sm = pltpu.make_async_copy(place_rx.at[group_rows], place_sm, sem_local.at[3])
    sm.start()
    wait_recv_all(place_rx.at[pl.ds(0, ND * (NG - 1))], sem_spread.at[1])

    hold_of = place_rx[...].reshape(N, 128).astype(F32)
    match = hold_of == expert_row
    dev_ids = iota((N, PAIRS), 0).astype(F32)
    holder = jnp.sum(jnp.where(match, dev_ids, 0.0), axis=0, keepdims=True)
    found = jnp.sum(jnp.where(match, 1.0, 0.0), axis=0, keepdims=True)
    use_copy = (replica_row > 0.5) & (found > 0.5)
    home = jnp.floor(expert_row * 0.5)
    target = jnp.where(use_copy, holder, home)
    slot = jnp.where(use_copy, float(HOLD), expert_row - 2.0 * home)
    target_col = to_col(target)
    slot_col = to_col(slot)
    earlier = (target_col == target) & (iota((PAIRS, PAIRS), 0) < iota((PAIRS, PAIRS), 1))
    position = jnp.sum(jnp.where(earlier, 1.0, 0.0), axis=0, keepdims=True)
    cell = jnp.where(position < CAP, target * CAP + position, -1.0)
    placed = jnp.where(iota((CELLS, PAIRS), 0).astype(F32) == cell, 1.0, 0.0)
    cell_col = jnp.concatenate([to_col(cell)] * 2, axis=1)
    placed_t[...] = jnp.where(iota((PAIRS, CELLS), 1).astype(F32) == cell_col, 1.0, 0.0).astype(BF)
    placed = placed.astype(BF)
    to_rows = (iota((PAIRS, ROWS), 0) // TOPK == iota((PAIRS, ROWS), 1)).astype(BF)
    row_pick = jnp.dot(placed, to_rows, preferred_element_type=F32).astype(BF)

    @pl.loop(0, D // 512)
    def _(i):
        cols = pl.ds(pl.multiple_of(i * 512, 512), 512)
        big[:, cols] = jnp.dot(row_pick, tokens[:, cols], preferred_element_type=F32)

    big[:, D:] = jnp.dot(placed, (slot_col + 1.0).astype(BF), preferred_element_type=F32) - 1.0

    unpack_rows(big, tx)

    for i in range(1, NG):
        t = across(i)
        remote(
            tx.at[pl.ds(pl.multiple_of(t * ND, ND), ND)], mid.at[g], sem_tok.at[0], sem_tok.at[1], (t, d)
        ).start()
    mid_own = pltpu.make_async_copy(tx.at[group_rows], mid.at[g], sem_local.at[8])
    mid_own.start()
    supply_steps((0, 1), EARLY, 3)
    supply_sends((0,), 3 * SUB)
    mid_own.wait()
    wait_recv_all(mid.at[pl.ds(0, NG - 1)], sem_tok.at[1])
    for o in ORDER:
        p = peer(o)
        remote(mid.at[:, p], rx.at[d], sem_tok2.at[0], sem_tok2.at[1], (g, p)).start()
    tok_own = pltpu.make_async_copy(mid.at[:, d], rx.at[d], sem_local.at[4])
    tok_own.start()
    supply_steps((2, 3), 0, 3)
    supply_sends((2,), 3 * SUB)


    def wanted(axis, u, v):
        w = place_sm[dev_of(axis, u, v), 0, 0]
        s = lax.rem(w // HOLD, ND)
        su, sv = (s // 4, lax.rem(s, 4)) if axis == 0 else (lax.rem(s, 4), s // 4)
        return su, sv, lax.rem(w, HOLD)

    def entry_of(role, u, want):
        su, sv, m = want
        line = (su == u).astype(I32) if role == 0 else (su != u).astype(I32)
        return role * 16 + (line * 4 + sv) * 2 + m

    def trade(k):
        _, _, _, rows, axis = CHUNKS[k]
        u, v = place_of(axis)
        for cp in own[k]:
            cp.wait()
        wait_recv_all(relays[k].at[pl.ds(0, 28)], sem_1r.at[k])
        for role in range(2):
            @pl.loop(0, 8)
            def _(j, role=role):
                line = mod4(u + (1 if role == 0 else -2) + j // 4)
                want = wanted(axis, line, lax.rem(j, 4))
                sends[k][role * 8 + j] = relays[k][entry_of(role, u, want)]

        @pl.loop(0, 8)
        def _(j):
            for role in range(2):
                to = dev_of(axis, mod4(u + (1 if role == 0 else -1)), v)
                remote(
                    sends[k].at[role * 8 + j], swaps[k].at[(1 - role) * 8 + j], sem_2s.at[k], sem_2r.at[k], (g, to)
                ).start()

    def landing(k, role):
        f, _, base, rows, axis = CHUNKS[k]
        u, v = place_of(axis)
        c = u if role == 0 else mod4(u - 1)
        return w_new.at[f, piece_rows(c, base, rows), pl.ds(pl.multiple_of(v * 128, 128), 128)]

    def own_slot(axis, role):
        _, v = place_of(axis)
        return role * 8 + (4 if role == 0 else 0) + v

    def deliver(k):
        _, _, _, rows, axis = CHUNKS[k]
        u, v = place_of(axis)
        wait_recv_all(swaps[k], sem_2r.at[k])
        wait_recv_all(sends[k], sem_2s.at[k])
        for role in range(2):
            @pl.loop(0, 8)
            def _(j, role=role):
                line = mod4(u + (-1 if role == 0 else 0) + j // 4)
                want = wanted(axis, line, lax.rem(j, 4))
                near = (want[0] == u) | (want[0] == mod4(u + (-1 if role == 0 else 1)))
                mine = relays[k][entry_of(role, u, want)]
                other = swaps[k][role * 8 + j]
                sends[k][role * 8 + j] = jnp.where(near, mine, other)
        for dv, role, line in (
            (1, 0, 1), (3, 0, 1), (0, 0, 0), (0, 1, 1), (1, 1, 0), (3, 1, 0), (1, 0, 0), (3, 1, 1),
            (3, 0, 0), (1, 1, 1), (2, 0, 1), (2, 1, 1), (2, 1, 0), (2, 0, 0),
        ):
            r = mod4(v + dv)
            to = dev_of(axis, mod4(u + line - (1 if role == 0 else 0)), r)
            remote(
                sends[k].at[role * 8 + line * 4 + r], landing(k, role), sem_3s.at[k], sem_3r.at[k], (g, to)
            ).start()
        for role in range(2):
            pltpu.make_async_copy(
                sends[k].at[own_slot(axis, role)], landing(k, role), sem_own3.at[k, role]
            ).start()

    def delivered(k):
        for role in range(2):
            pltpu.make_async_copy(
                sends[k].at[own_slot(CHUNKS[k][4], role)], landing(k, role), sem_own3.at[k, role]
            ).wait()
        got = w_new.at[0, pl.ds(0, 14 * CHUNKS[k][3] // 4), :]
        pltpu.make_async_copy(got, got, sem_3r.at[k]).wait()

    sm.wait()

    meta_own.wait()
    wait_recv_all(meta_rx.at[pl.ds(0, ND - 1)], sem_meta.at[1])
    mine_w = place[0]
    got = meta_rx[lax.rem(mine_w // HOLD, ND)]
    slot_m = lax.rem(mine_w, HOLD)
    got_wide = got.astype(F32)
    mine_scales = jnp.where(slot_m == 0, got_wide[0:8], got_wide[8:16])
    scale_out[...] = mine_scales[:, 0:KT].astype(BF)

    def grow_scales(block, m, f):
        tiles = 2 * (iota((128, HALF), 1) // TILE) + f
        sel = (iota((128, HALF), 0) == tiles + 8 * m).astype(BF)
        tall = jnp.concatenate([block.astype(F32), jnp.zeros((112, 128), F32)], axis=0).T
        return jnp.dot(tall[0:32].astype(BF), sel, preferred_element_type=F32).reshape(32, 1, HALF)

    for f in range(2):
        for m in range(HOLD):
            grow[m, f] = grow_scales(meta_tx[...], m, f)
        grow[HOLD, f] = grow_scales(got, slot_m, f)

    tok_own.wait()
    wait_recv_all(rx.at[pl.ds(0, ND - 1)], sem_tok2.at[1])

    pack_rows(rx, big, True)

    code = big[:, D:]
    load_row = jnp.zeros((1, 128), F32)
    for s in range(HOLD + 1):
        count = jnp.sum(jnp.where(code == float(s), 1.0, 0.0), axis=0, keepdims=True)
        load_row = jnp.where(iota((1, 128), 1) == s, count, load_row)
    load_out[...] = load_row[:, 0 : HOLD + 1].astype(I32)

    for s in range(HOLD + 1):
        @pl.loop(0, KT)
        def _(k, s=s):
            cols = pl.ds(pl.multiple_of(k * TILE, TILE), TILE)
            xm[s, :, cols] = jnp.where(code == float(s), big[:, cols], 0.0).astype(BF)

    acc[...] = jnp.zeros((2, CELLS, HALF), F32)
    n_q = HOLD * (D // QROWS)

    @pl.loop(0, n_q)
    def _(i):
        @pl.when(i + 1 < n_q)
        def _():
            q_copy(i + 1).start()
        q_copy(i).wait()
        m = i // (D // QROWS)
        tile0 = lax.rem(i, D // QROWS) * (QROWS // TILE)
        xs = xm[m, :, pl.ds(pl.multiple_of(tile0 * TILE, TILE), QROWS)]
        for f in range(2):
            cols = [qbuf[lax.rem(i, 2), :, 256 * r + 128 * f : 256 * r + 128 * f + 128] for r in range(4)]
            w = jnp.concatenate(cols, axis=1).astype(F32).reshape(QROWS // TILE, TILE, HALF)
            w = (w * grow[m, f, pl.ds(tile0, QROWS // TILE)]).astype(BF).reshape(QROWS, HALF)
            acc[f] += jnp.dot(xs, w, preferred_element_type=F32)

    trade(0)
    trade(1)
    deliver(0)
    trade(2)
    deliver(1)
    trade(3)
    deliver(2)
    deliver(3)

    def serve(k):
        f, _, base, rows, _ = CHUNKS[k]
        delivered(k)

        @pl.loop(0, 4)
        def _(c):
            at = piece_rows(c, base, rows)
            tile0 = c * (PIECE // TILE) + base // TILE
            w = w_new[f, at, :].astype(F32).reshape(rows // TILE, TILE, HALF)
            w = (w * grow[HOLD, f, pl.ds(tile0, rows // TILE)]).astype(BF).reshape(rows, HALF)
            acc[f] += jnp.dot(xm[HOLD, :, at], w, preferred_element_type=F32)

    def write_out(f, r):
        return pltpu.make_async_copy(
            w_new.at[f, :, pl.ds(r * 128, 128)], w_out.at[:, pl.ds(r * 256 + f * 128, 128)], sem_w.at[f, r]
        )

    def back_rows(p):
        return pl.ds(pl.multiple_of(p * NG, NG), NG)

    def finish(f):
        for r in range(4):
            write_out(f, r).start()
        v = acc[f]
        acc[f] = v / (1.0 + jnp.exp(-v))
        unpack_rows(acc.at[f], back_tx.at[f])
        for o in ORDER:
            p = peer(o)
            remote(
                back_tx.at[f, back_rows(p)], back_mid.at[f, :, d], sem_ret.at[f, 0], sem_ret.at[f, 1], (g, peer(o))
            ).start()
        back_copy(f).start()

    def back_copy(f):
        return pltpu.make_async_copy(back_tx.at[f, back_rows(d)], back_mid.at[f, :, d], sem_local.at[5 + f])

    def back_own(f):
        return pltpu.make_async_copy(back_mid.at[f, g], back_rx.at[f, group_rows], sem_local.at[9 + f])

    def back_across(f):
        back_copy(f).wait()
        wait_recv_all(back_mid.at[f, :, pl.ds(0, ND - 1)], sem_ret.at[f, 1])
        for i in range(1, NG):
            t = across(i)
            remote(
                back_mid.at[f, t], back_rx.at[f, group_rows], sem_ret2.at[f, 0], sem_ret2.at[f, 1], (t, d)
            ).start()
        back_own(f).start()

    def arrive(f):
        back_own(f).wait()
        wait_recv_all(back_rx.at[f, pl.ds(0, ND * (NG - 1))], sem_ret2.at[f, 1])
        pack_rows(back_rx.at[f], acc.at[f])
        part = jnp.dot(placed_t[...], acc[f].astype(BF), preferred_element_type=F32)
        part = (part * weight_col[:, 0:1]).astype(BF)
        for r in range(4):
            hidden_out[:, 256 * r + 128 * f : 256 * r + 128 * f + 128] = part[:, 128 * r : 128 * r + 128]

    serve(0)
    serve(1)
    finish(0)
    serve(2)
    back_across(0)
    serve(3)
    finish(1)
    arrive(0)
    back_across(1)
    arrive(1)

    wait_recv_all(place_rx.at[pl.ds(0, ND - 1)], sem_place.at[0])
    wait_recv_all(place_rx.at[pl.ds(0, ND * (NG - 1))], sem_spread.at[0])
    wait_recv_all(meta_rx.at[pl.ds(0, ND - 1)], sem_meta.at[0])
    for k in range(4):
        wait_recv_all(relays[k].at[pl.ds(0, 28)], sem_1s.at[k])
        wait_recv_all(sends[k].at[pl.ds(0, 14)], sem_3s.at[k])
    wait_recv_all(mid.at[pl.ds(0, NG - 1)], sem_tok.at[0])
    wait_recv_all(rx.at[pl.ds(0, ND - 1)], sem_tok2.at[0])
    for f in range(2):
        wait_recv_all(back_mid.at[f, :, pl.ds(0, ND - 1)], sem_ret.at[f, 0])
        wait_recv_all(back_rx.at[f, pl.ds(0, ND * (NG - 1))], sem_ret2.at[f, 0])
        for r in range(4):
            write_out(f, r).wait()


def per_device(primary_q, primary_scales, new_place, tokens, experts, replica, route_num):
    vmem = pl.BlockSpec(memory_space=pltpu.VMEM)
    anywhere = pl.BlockSpec(memory_space=pl.ANY)
    dma = pltpu.SemaphoreType.DMA
    scratch = [
        pltpu.VMEM((1, 128), I32),
        pltpu.VMEM((N, 1, 128), I32),
        pltpu.SMEM((ND, 1, 128), I32),
        pltpu.VMEM((16, 128), BF),
        pltpu.VMEM((ND, 16, 128), BF),
        *[pltpu.VMEM((32, c[3], 128), BF) for c in CHUNKS],
        *[pltpu.VMEM((16, c[3], 128), BF) for c in CHUNKS],
        *[pltpu.VMEM((16, c[3], 128), BF) for c in CHUNKS],
        pltpu.VMEM((2, D, HALF), BF),
        pltpu.VMEM((CELLS, WIDE), F32),
        pltpu.VMEM((N, CAP, WIDE), BF),
        pltpu.VMEM((NG, ND, CAP, WIDE), BF),
        pltpu.VMEM((ND, NG, CAP, WIDE), BF),
        pltpu.VMEM((HOLD + 1, CELLS, D), BF),
        pltpu.VMEM((2, CELLS, HALF), F32),
        pltpu.VMEM((2, N, CAP, HALF), BF),
        pltpu.VMEM((2, NG, ND, CAP, HALF), BF),
        pltpu.VMEM((2, N, CAP, HALF), BF),
        pltpu.VMEM((2, QROWS, FF), BF),
        pltpu.VMEM((HOLD + 1, 2, 32, 1, HALF), F32),
        pltpu.VMEM((PAIRS, CELLS), BF),
        dma((2,)), dma((2,)), dma((2,)), dma((4,)), dma((4,)), dma((4,)), dma((4,)), dma((4,)), dma((4,)),
        dma((4, 2)), dma((4, 2)),
        dma((2,)), dma((2,)), dma((2, 2)), dma((2, 2)), dma((11,)), dma((2,)), dma((2, 4)),
    ]
    new_weights, scale_tile, hidden, load = pl.pallas_call(
        kernel,
        out_shape=(
            jax.ShapeDtypeStruct((D, FF), BF),
            jax.ShapeDtypeStruct((8, KT), BF),
            jax.ShapeDtypeStruct((PAIRS, FF), BF),
            jax.ShapeDtypeStruct((1, HOLD + 1), I32),
        ),
        in_specs=[
            anywhere, vmem, pl.BlockSpec(memory_space=pltpu.SMEM), vmem, vmem, vmem, vmem,
        ],
        out_specs=(anywhere, vmem, vmem, vmem),
        scratch_shapes=scratch,
        compiler_params=pltpu.CompilerParams(
            collective_id=0, has_side_effects=True, vmem_limit_bytes=64000 * 1024
        ),
    )(
        primary_q, primary_scales.transpose(0, 2, 1), new_place, tokens,
        experts.T, replica.T, route_num.T,
    )
    return (
        new_weights.reshape(1, D, FF),
        scale_tile.T.reshape(1, KT, 8),
        hidden.reshape(ROWS, TOPK, FF),
        load,
    )


def solution(mesh):
    both = ("group", "dev")
    return jax.shard_map(
        per_device,
        mesh=mesh,
        in_specs=(
            P(both, None, None), P(both, None, None), P(both), P(both, None),
            P(both, None), P(both, None), P(both, None),
        ),
        out_specs=(P(both, None, None), P(both, None, None), P(both, None, None), P(both, None)),
        check_vma=False,
    )
```

```python
import jax
import jax.numpy as jnp
from jax import lax
from jax.experimental import pallas as pl
from jax.experimental.pallas import tpu as pltpu
from jax.sharding import PartitionSpec as P

D = 3584
FF = 1024
TILE = 128
CAP = 2
HOLD = 2
NG = 8
ND = 16
N = NG * ND
ROWS = 16
TOPK = 8
PAIRS = ROWS * TOPK
CELLS = N * CAP
KT = D // TILE
WIDE = D + 128
BF = jnp.bfloat16
F32 = jnp.float32
I32 = jnp.int32
MESH = pl.DeviceIdType.MESH

ORDER = (
    (0, 1), (0, 3), (1, 0), (3, 0), (1, 1), (3, 3), (1, 3), (3, 1),
    (0, 2), (2, 0), (2, 2), (1, 2), (3, 2), (2, 1), (2, 3),
)
CHUNKS = ((0, 0, 0, 512, 0), (0, 1, 512, 384, 1), (1, 0, 0, 512, 1), (1, 1, 512, 384, 0))
PIECE = 896
HALF = 512
SUB = 64
EARLY = 4
QROWS = 512


def iota(shape, dim):
    return lax.broadcasted_iota(I32, shape, dim)


def unpack_rows(flat, blocks):
    @pl.loop(0, CELLS // 8)
    def _(i):
        v = flat[pl.ds(pl.multiple_of(8 * i, 8), 8), :]
        for j in range(4):
            blocks[4 * i + j] = v[2 * j : 2 * j + 2].astype(BF)


def pack_rows(blocks, flat, nested=False):
    @pl.loop(0, CELLS // 8)
    def _(i):
        at = [(i // 2, lax.rem(i, 2) * 4 + j) if nested else (4 * i + j,) for j in range(4)]
        v = [blocks[a].astype(F32) for a in at]
        flat[pl.ds(pl.multiple_of(8 * i, 8), 8), :] = jnp.concatenate(v, axis=0)


def kernel(
    q, scales, place, tokens, experts, replica, route,
    w_new, scale_out, hidden_out, load_out,
    place_tx, place_rx, place_sm, meta_tx, meta_rx,
    r0, r1, r2, r3, y0, y1, y2, y3, s0, s1, s2, s3,
    big, tx, mid, rx, xm, acc, back_tx, back_mid, back_rx, qbuf, grow, placed_t,
    sem_place, sem_spread, sem_meta, sem_1s, sem_1r, sem_2s, sem_2r, sem_3s, sem_3r, sem_own1, sem_own3,
    sem_tok, sem_tok2, sem_ret, sem_ret2, sem_local, sem_q,
):
    g = lax.axis_index("group")
    d = lax.axis_index("dev")
    z, x = d // 4, d % 4
    me = g * ND + d

    def peer(o):
        return lax.rem(z + o[0], 4) * 4 + lax.rem(x + o[1], 4)

    def remote(src, dst, ssem, rsem, dev):
        return pltpu.make_async_remote_copy(
            src_ref=src, dst_ref=dst, send_sem=ssem, recv_sem=rsem,
            device_id=dev, device_id_type=MESH,
        )

    def across(i):
        return lax.rem(g + i, NG)

    place_tx[...] = jnp.full((1, 128), place[0], I32)
    place_rx[me] = jnp.full((1, 128), place[0], I32)
    widen = (iota((KT, 128), 0) == iota((KT, 128), 1)).astype(BF)
    spread = [jnp.dot(scales[m], widen, preferred_element_type=F32) for m in range(HOLD)]
    meta_tx[...] = jnp.concatenate(spread, axis=0).astype(BF)

    barrier = pltpu.get_barrier_semaphore()

    for o in ORDER:
        pl.semaphore_signal(barrier, inc=1, device_id=(g, peer(o)), device_id_type=MESH)
    for i in range(1, NG):
        pl.semaphore_signal(barrier, inc=1, device_id=(across(i), d), device_id_type=MESH)
    pl.semaphore_wait(barrier, ND - 1 + NG - 1)

    for o in ORDER:
        remote(place_tx, place_rx.at[me], sem_place.at[0], sem_place.at[1], (g, peer(o))).start()
    for o in ORDER:
        remote(meta_tx, meta_rx.at[d], sem_meta.at[0], sem_meta.at[1], (g, peer(o))).start()
    meta_own = pltpu.make_async_copy(meta_tx, meta_rx.at[d], sem_local.at[0])
    meta_own.start()

    relays = (r0, r1, r2, r3)
    swaps = (y0, y1, y2, y3)
    sends = (s0, s1, s2, s3)

    def place_of(axis):
        return (z, x) if axis == 0 else (x, z)

    def dev_of(axis, u, v):
        return u * 4 + v if axis == 0 else v * 4 + u

    def mod4(i):
        return lax.rem(i + 8, 4)

    def piece_rows(c, first, n):
        return pl.ds(pl.multiple_of(c * PIECE + first, SUB), n)

    def piece_cols(r, f):
        return pl.ds(pl.multiple_of(r * 256 + f * 128, 128), 128)

    KINDS = ((0, 0, 0, 1), (0, 1, -1, 0), (1, 0, 1, 0), (-1, 1, -2, 1))
    FIRST = ((1, 0), (3, 0), (0, 2), (0, 3), (1, 1), (3, 1), (1, 2), (3, 3), (3, 2), (1, 3), (2, 0), (2, 2), (2, 1), (2, 3))

    def supply(k, dv, kind, at, n):
        f, _, base, rows, axis = CHUNKS[k]
        u, v = place_of(axis)
        step, role, piece, line = KINDS[kind]
        r = mod4(v + dv)
        src = q.at[:, piece_rows(mod4(u + piece), base + at, n), piece_cols(r, f)]
        entry = role * 16 + (line * 4 + v) * 2
        dst = relays[k].at[pl.ds(entry, 2), pl.ds(pl.multiple_of(at, SUB), n)]
        return src, dst, (g, dev_of(axis, mod4(u + step), r))

    def supply_sends(ks, at):
        for dv, kind in FIRST:
            for k in ks:
                src, dst, dev = supply(k, dv, kind, at, SUB)
                remote(src, dst, sem_1s.at[k], sem_1r.at[k], dev).start()

    def supply_own(k):
        cps = []
        for kind in range(2):
            src, dst, _ = supply(k, 0, kind, 0, CHUNKS[k][3])
            cps.append(pltpu.make_async_copy(src, dst, sem_own1.at[k, kind]))
        return cps

    def supply_steps(pair, lo, hi):
        @pl.loop(lo, hi)
        def _(i):
            supply_sends(pair, i * SUB)

    supply_steps((0, 1), 0, EARLY)
    own = [supply_own(k) for k in range(4)]
    for cps in own:
        for cp in cps:
            cp.start()

    def q_copy(i):
        return pltpu.make_async_copy(
            q.at[i // (D // QROWS), pl.ds(pl.multiple_of(lax.rem(i, D // QROWS) * QROWS, QROWS), QROWS)],
            qbuf.at[lax.rem(i, 2)], sem_q.at[lax.rem(i, 2)],
        )

    q_copy(0).start()

    def to_row(a):
        rep = (iota((ROWS, PAIRS), 1) // TOPK == iota((ROWS, PAIRS), 0)).astype(BF)
        wide = jnp.dot(a[...].astype(F32).astype(BF), rep, preferred_element_type=F32)
        mine = lax.rem(iota((TOPK, PAIRS), 1), TOPK) == iota((TOPK, PAIRS), 0)
        return jnp.sum(jnp.where(mine, wide, 0.0), axis=0, keepdims=True)

    def to_col(row):
        return jnp.broadcast_to(row, (PAIRS, PAIRS)).T

    expert_row = to_row(experts)
    replica_row = to_row(replica)
    weight_col = to_col(to_row(route) * (1.0 / 16.0))

    def wait_recv_all(ref, sem):
        pltpu.make_async_copy(ref, ref, sem).wait()

    group_rows = pl.ds(pl.multiple_of(g * ND, ND), ND)
    wait_recv_all(place_rx.at[pl.ds(0, ND - 1)], sem_place.at[1])
    for i in range(1, NG):
        remote(
            place_rx.at[group_rows], place_rx.at[group_rows], sem_spread.at[0], sem_spread.at[1], (across(i), d)
        ).start()
    sm = pltpu.make_async_copy(place_rx.at[group_rows], place_sm, sem_local.at[3])
    sm.start()
    wait_recv_all(place_rx.at[pl.ds(0, ND * (NG - 1))], sem_spread.at[1])

    hold_of = place_rx[...].reshape(N, 128).astype(F32)
    match = hold_of == expert_row
    dev_ids = iota((N, PAIRS), 0).astype(F32)
    holder = jnp.sum(jnp.where(match, dev_ids, 0.0), axis=0, keepdims=True)
    found = jnp.sum(jnp.where(match, 1.0, 0.0), axis=0, keepdims=True)
    use_copy = (replica_row > 0.5) & (found > 0.5)
    home = jnp.floor(expert_row * 0.5)
    target = jnp.where(use_copy, holder, home)
    slot = jnp.where(use_copy, float(HOLD), expert_row - 2.0 * home)
    target_col = to_col(target)
    slot_col = to_col(slot)
    earlier = (target_col == target) & (iota((PAIRS, PAIRS), 0) < iota((PAIRS, PAIRS), 1))
    position = jnp.sum(jnp.where(earlier, 1.0, 0.0), axis=0, keepdims=True)
    cell = jnp.where(position < CAP, target * CAP + position, -1.0)
    placed = jnp.where(iota((CELLS, PAIRS), 0).astype(F32) == cell, 1.0, 0.0)
    cell_col = jnp.concatenate([to_col(cell)] * 2, axis=1)
    placed_t[...] = jnp.where(iota((PAIRS, CELLS), 1).astype(F32) == cell_col, 1.0, 0.0).astype(BF)
    placed = placed.astype(BF)
    to_rows = (iota((PAIRS, ROWS), 0) // TOPK == iota((PAIRS, ROWS), 1)).astype(BF)
    row_pick = jnp.dot(placed, to_rows, preferred_element_type=F32).astype(BF)

    @pl.loop(0, D // 512)
    def _(i):
        cols = pl.ds(pl.multiple_of(i * 512, 512), 512)
        big[:, cols] = jnp.dot(row_pick, tokens[:, cols], preferred_element_type=F32)

    big[:, D:] = jnp.dot(placed, (slot_col + 1.0).astype(BF), preferred_element_type=F32) - 1.0

    unpack_rows(big, tx)

    for i in range(1, NG):
        t = across(i)
        remote(
            tx.at[pl.ds(pl.multiple_of(t * ND, ND), ND)], mid.at[g], sem_tok.at[0], sem_tok.at[1], (t, d)
        ).start()
    mid_own = pltpu.make_async_copy(tx.at[group_rows], mid.at[g], sem_local.at[8])
    mid_own.start()
    supply_steps((0, 1), EARLY, 6)
    supply_steps((0,), 6, 8)
    mid_own.wait()
    wait_recv_all(mid.at[pl.ds(0, NG - 1)], sem_tok.at[1])
    for o in ORDER:
        p = peer(o)
        remote(mid.at[:, p], rx.at[d], sem_tok2.at[0], sem_tok2.at[1], (g, p)).start()
    tok_own = pltpu.make_async_copy(mid.at[:, d], rx.at[d], sem_local.at[4])
    tok_own.start()
    supply_steps((2, 3), 0, 6)
    supply_steps((2,), 6, 8)


    def wanted(axis, u, v):
        w = place_sm[dev_of(axis, u, v), 0, 0]
        s = lax.rem(w // HOLD, ND)
        su, sv = (s // 4, lax.rem(s, 4)) if axis == 0 else (lax.rem(s, 4), s // 4)
        return su, sv, lax.rem(w, HOLD)

    def entry_of(role, u, want):
        su, sv, m = want
        line = (su == u).astype(I32) if role == 0 else (su != u).astype(I32)
        return role * 16 + (line * 4 + sv) * 2 + m

    def trade_pick(k):
        _, _, _, rows, axis = CHUNKS[k]
        u, v = place_of(axis)
        for cp in own[k]:
            cp.wait()
        wait_recv_all(relays[k].at[pl.ds(0, 28)], sem_1r.at[k])
        for role in range(2):
            @pl.loop(0, 8)
            def _(j, role=role):
                line = mod4(u + (1 if role == 0 else -2) + j // 4)
                want = wanted(axis, line, lax.rem(j, 4))
                sends[k][role * 8 + j] = relays[k][entry_of(role, u, want)]

    def trade(pair):
        for k in pair:
            trade_pick(k)

        @pl.loop(0, 8)
        def _(j):
            for role in range(2):
                for k in pair:
                    axis = CHUNKS[k][4]
                    u, v = place_of(axis)
                    to = dev_of(axis, mod4(u + (1 if role == 0 else -1)), v)
                    remote(
                        sends[k].at[role * 8 + j], swaps[k].at[(1 - role) * 8 + j],
                        sem_2s.at[k], sem_2r.at[k], (g, to),
                    ).start()

    def landing(k, role):
        f, _, base, rows, axis = CHUNKS[k]
        u, v = place_of(axis)
        c = u if role == 0 else mod4(u - 1)
        return w_new.at[piece_rows(c, base, rows), piece_cols(v, f)]

    LAST = (
        (1, 0, 1), (3, 0, 1), (0, 0, 0), (0, 1, 1), (1, 1, 0), (3, 1, 0), (1, 0, 0), (3, 1, 1),
        (3, 0, 0), (1, 1, 1), (2, 0, 1), (2, 1, 1), (2, 1, 0), (2, 0, 0),
    )

    def own_slot(axis, role):
        _, v = place_of(axis)
        return role * 8 + (4 if role == 0 else 0) + v

    def deliver_pick(k):
        _, _, _, rows, axis = CHUNKS[k]
        u, v = place_of(axis)
        wait_recv_all(swaps[k], sem_2r.at[k])
        wait_recv_all(sends[k], sem_2s.at[k])
        for role in range(2):
            @pl.loop(0, 8)
            def _(j, role=role):
                line = mod4(u + (-1 if role == 0 else 0) + j // 4)
                want = wanted(axis, line, lax.rem(j, 4))
                near = (want[0] == u) | (want[0] == mod4(u + (-1 if role == 0 else 1)))
                mine = relays[k][entry_of(role, u, want)]
                other = swaps[k][role * 8 + j]
                sends[k][role * 8 + j] = jnp.where(near, mine, other)
        for role in range(2):
            pltpu.make_async_copy(
                sends[k].at[own_slot(axis, role)], landing(k, role), sem_own3.at[k, role]
            ).start()

    def deliver(pair):
        for k in pair:
            deliver_pick(k)
        for dv, role, line in LAST:
            for k in pair:
                axis = CHUNKS[k][4]
                u, v = place_of(axis)
                r = mod4(v + dv)
                to = dev_of(axis, mod4(u + line - (1 if role == 0 else 0)), r)
                remote(
                    sends[k].at[role * 8 + line * 4 + r], landing(k, role), sem_3s.at[k], sem_3r.at[k], (g, to)
                ).start()

    def delivered(k):
        for role in range(2):
            pltpu.make_async_copy(
                sends[k].at[own_slot(CHUNKS[k][4], role)], landing(k, role), sem_own3.at[k, role]
            ).wait()
        got = w_new.at[pl.ds(0, 14 * CHUNKS[k][3] // 8), :]
        pltpu.make_async_copy(got, got, sem_3r.at[k]).wait()

    sm.wait()

    meta_own.wait()
    wait_recv_all(meta_rx.at[pl.ds(0, ND - 1)], sem_meta.at[1])
    mine_w = place[0]
    got = meta_rx[lax.rem(mine_w // HOLD, ND)]
    slot_m = lax.rem(mine_w, HOLD)
    got_wide = got.astype(F32)
    mine_scales = jnp.where(slot_m == 0, got_wide[0:8], got_wide[8:16])
    scale_out[...] = mine_scales[:, 0:KT].astype(BF)

    def grow_scales(block, m, f):
        tiles = 2 * (iota((128, HALF), 1) // TILE) + f
        sel = (iota((128, HALF), 0) == tiles + 8 * m).astype(BF)
        tall = jnp.concatenate([block.astype(F32), jnp.zeros((112, 128), F32)], axis=0).T
        return jnp.dot(tall[0:32].astype(BF), sel, preferred_element_type=F32).reshape(32, 1, HALF)

    for f in range(2):
        for m in range(HOLD):
            grow[m, f] = grow_scales(meta_tx[...], m, f)
        grow[HOLD, f] = grow_scales(got, slot_m, f)

    tok_own.wait()
    wait_recv_all(rx.at[pl.ds(0, ND - 1)], sem_tok2.at[1])

    pack_rows(rx, big, True)

    code = big[:, D:]
    load_row = jnp.zeros((1, 128), F32)
    for s in range(HOLD + 1):
        count = jnp.sum(jnp.where(code == float(s), 1.0, 0.0), axis=0, keepdims=True)
        load_row = jnp.where(iota((1, 128), 1) == s, count, load_row)
    load_out[...] = load_row[:, 0 : HOLD + 1].astype(I32)

    for s in range(HOLD + 1):
        @pl.loop(0, KT)
        def _(k, s=s):
            cols = pl.ds(pl.multiple_of(k * TILE, TILE), TILE)
            xm[s, :, cols] = jnp.where(code == float(s), big[:, cols], 0.0).astype(BF)

    acc[...] = jnp.zeros((2, CELLS, HALF), F32)
    n_q = HOLD * (D // QROWS)

    @pl.loop(0, n_q)
    def _(i):
        @pl.when(i + 1 < n_q)
        def _():
            q_copy(i + 1).start()
        q_copy(i).wait()
        m = i // (D // QROWS)
        tile0 = lax.rem(i, D // QROWS) * (QROWS // TILE)
        xs = xm[m, :, pl.ds(pl.multiple_of(tile0 * TILE, TILE), QROWS)]
        for f in range(2):
            cols = [qbuf[lax.rem(i, 2), :, 256 * r + 128 * f : 256 * r + 128 * f + 128] for r in range(4)]
            w = jnp.concatenate(cols, axis=1).astype(F32).reshape(QROWS // TILE, TILE, HALF)
            w = (w * grow[m, f, pl.ds(tile0, QROWS // TILE)]).astype(BF).reshape(QROWS, HALF)
            acc[f] += jnp.dot(xs, w, preferred_element_type=F32)

    trade((0, 1))
    trade((2, 3))
    deliver((0, 1))
    deliver((2, 3))

    def serve(k):
        f, _, base, rows, _ = CHUNKS[k]
        delivered(k)

        @pl.loop(0, 4)
        def _(c):
            at = piece_rows(c, base, rows)
            tile0 = c * (PIECE // TILE) + base // TILE
            cols = [w_new[at, 256 * r + 128 * f : 256 * r + 128 * f + 128] for r in range(4)]
            w = jnp.concatenate(cols, axis=1).astype(F32).reshape(rows // TILE, TILE, HALF)
            w = (w * grow[HOLD, f, pl.ds(tile0, rows // TILE)]).astype(BF).reshape(rows, HALF)
            acc[f] += jnp.dot(xm[HOLD, :, at], w, preferred_element_type=F32)

    def back_rows(p):
        return pl.ds(pl.multiple_of(p * NG, NG), NG)

    def finish(f):
        v = acc[f]
        acc[f] = v / (1.0 + jnp.exp(-v))
        unpack_rows(acc.at[f], back_tx.at[f])
        for o in ORDER:
            p = peer(o)
            remote(
                back_tx.at[f, back_rows(p)], back_mid.at[f, :, d], sem_ret.at[f, 0], sem_ret.at[f, 1], (g, peer(o))
            ).start()
        back_copy(f).start()

    def back_copy(f):
        return pltpu.make_async_copy(back_tx.at[f, back_rows(d)], back_mid.at[f, :, d], sem_local.at[5 + f])

    def back_own(f):
        return pltpu.make_async_copy(back_mid.at[f, g], back_rx.at[f, group_rows], sem_local.at[9 + f])

    def back_across(f):
        back_copy(f).wait()
        wait_recv_all(back_mid.at[f, :, pl.ds(0, ND - 1)], sem_ret.at[f, 1])
        for i in range(1, NG):
            t = across(i)
            remote(
                back_mid.at[f, t], back_rx.at[f, group_rows], sem_ret2.at[f, 0], sem_ret2.at[f, 1], (t, d)
            ).start()
        back_own(f).start()

    def arrive(f):
        back_own(f).wait()
        wait_recv_all(back_rx.at[f, pl.ds(0, ND * (NG - 1))], sem_ret2.at[f, 1])
        pack_rows(back_rx.at[f], acc.at[f])
        part = jnp.dot(placed_t[...], acc[f].astype(BF), preferred_element_type=F32)
        part = (part * weight_col[:, 0:1]).astype(BF)
        for r in range(4):
            hidden_out[:, 256 * r + 128 * f : 256 * r + 128 * f + 128] = part[:, 128 * r : 128 * r + 128]

    serve(0)
    serve(1)
    finish(0)
    serve(2)
    back_across(0)
    serve(3)
    finish(1)
    arrive(0)
    back_across(1)
    arrive(1)

    wait_recv_all(place_rx.at[pl.ds(0, ND - 1)], sem_place.at[0])
    wait_recv_all(place_rx.at[pl.ds(0, ND * (NG - 1))], sem_spread.at[0])
    wait_recv_all(meta_rx.at[pl.ds(0, ND - 1)], sem_meta.at[0])
    for k in range(4):
        wait_recv_all(relays[k].at[pl.ds(0, 28)], sem_1s.at[k])
        wait_recv_all(sends[k].at[pl.ds(0, 14)], sem_3s.at[k])
    wait_recv_all(mid.at[pl.ds(0, NG - 1)], sem_tok.at[0])
    wait_recv_all(rx.at[pl.ds(0, ND - 1)], sem_tok2.at[0])
    for f in range(2):
        wait_recv_all(back_mid.at[f, :, pl.ds(0, ND - 1)], sem_ret.at[f, 0])
        wait_recv_all(back_rx.at[f, pl.ds(0, ND * (NG - 1))], sem_ret2.at[f, 0])


def per_device(primary_q, primary_scales, new_place, tokens, experts, replica, route_num):
    vmem = pl.BlockSpec(memory_space=pltpu.VMEM)
    anywhere = pl.BlockSpec(memory_space=pl.ANY)
    dma = pltpu.SemaphoreType.DMA
    scratch = [
        pltpu.VMEM((1, 128), I32),
        pltpu.VMEM((N, 1, 128), I32),
        pltpu.SMEM((ND, 1, 128), I32),
        pltpu.VMEM((16, 128), BF),
        pltpu.VMEM((ND, 16, 128), BF),
        *[pltpu.VMEM((32, c[3], 128), BF) for c in CHUNKS],
        *[pltpu.VMEM((16, c[3], 128), BF) for c in CHUNKS],
        *[pltpu.VMEM((16, c[3], 128), BF) for c in CHUNKS],
        pltpu.VMEM((CELLS, WIDE), F32),
        pltpu.VMEM((N, CAP, WIDE), BF),
        pltpu.VMEM((NG, ND, CAP, WIDE), BF),
        pltpu.VMEM((ND, NG, CAP, WIDE), BF),
        pltpu.VMEM((HOLD + 1, CELLS, D), BF),
        pltpu.VMEM((2, CELLS, HALF), F32),
        pltpu.VMEM((2, N, CAP, HALF), BF),
        pltpu.VMEM((2, NG, ND, CAP, HALF), BF),
        pltpu.VMEM((2, N, CAP, HALF), BF),
        pltpu.VMEM((2, QROWS, FF), BF),
        pltpu.VMEM((HOLD + 1, 2, 32, 1, HALF), F32),
        pltpu.VMEM((PAIRS, CELLS), BF),
        dma((2,)), dma((2,)), dma((2,)), dma((4,)), dma((4,)), dma((4,)), dma((4,)), dma((4,)), dma((4,)),
        dma((4, 2)), dma((4, 2)),
        dma((2,)), dma((2,)), dma((2, 2)), dma((2, 2)), dma((11,)), dma((2,)),
    ]
    new_weights, scale_tile, hidden, load = pl.pallas_call(
        kernel,
        out_shape=(
            pltpu.VMEM((D, FF), BF),
            pltpu.VMEM((8, KT), BF),
            pltpu.VMEM((PAIRS, FF), BF),
            pltpu.VMEM((1, HOLD + 1), I32),
        ),
        in_specs=[
            anywhere, vmem, pl.BlockSpec(memory_space=pltpu.SMEM), vmem, vmem, vmem, vmem,
        ],
        out_specs=(vmem, vmem, vmem, vmem),
        scratch_shapes=scratch,
        compiler_params=pltpu.CompilerParams(
            collective_id=0, has_side_effects=True, vmem_limit_bytes=56000 * 1024
        ),
    )(
        primary_q, primary_scales.transpose(0, 2, 1), new_place, tokens,
        experts.T, replica.T, route_num.T,
    )
    return (
        new_weights.reshape(1, D, FF),
        scale_tile.T.reshape(1, KT, 8),
        hidden.reshape(ROWS, TOPK, FF),
        load,
    )


def solution(mesh):
    both = ("group", "dev")
    return jax.shard_map(
        per_device,
        mesh=mesh,
        in_specs=(
            P(both, None, None), P(both, None, None), P(both), P(both, None),
            P(both, None), P(both, None), P(both, None),
        ),
        out_specs=(P(both, None, None), P(both, None, None), P(both, None, None), P(both, None)),
        check_vma=False,
    )
```

```python
import jax
import jax.numpy as jnp
from jax import lax
from jax.experimental import pallas as pl
from jax.experimental.pallas import tpu as pltpu
from jax.sharding import PartitionSpec as P

D = 3584
FF = 1024
TILE = 128
CAP = 2
HOLD = 2
NG = 8
ND = 16
N = NG * ND
ROWS = 16
TOPK = 8
PAIRS = ROWS * TOPK
CELLS = N * CAP
KT = D // TILE
WIDE = D + 128
BF = jnp.bfloat16
F32 = jnp.float32
I32 = jnp.int32
MESH = pl.DeviceIdType.MESH

ORDER = (
    (0, 1), (0, 3), (1, 0), (3, 0), (1, 1), (3, 3), (1, 3), (3, 1),
    (0, 2), (2, 0), (2, 2), (1, 2), (3, 2), (2, 1), (2, 3),
)
CHUNKS = ((0, 0, 0, 512, 0), (0, 1, 512, 384, 1), (1, 0, 0, 512, 1), (1, 1, 512, 384, 0))
PIECE = 896
HALF = 512
SUB = 64
EARLY = 4
QROWS = 512


def iota(shape, dim):
    return lax.broadcasted_iota(I32, shape, dim)


def unpack_rows(flat, blocks):
    @pl.loop(0, CELLS // 8)
    def _(i):
        v = flat[pl.ds(pl.multiple_of(8 * i, 8), 8), :]
        for j in range(4):
            blocks[4 * i + j] = v[2 * j : 2 * j + 2].astype(BF)


def pack_rows(blocks, flat, nested=False):
    @pl.loop(0, CELLS // 8)
    def _(i):
        at = [(i // 2, lax.rem(i, 2) * 4 + j) if nested else (4 * i + j,) for j in range(4)]
        v = [blocks[a].astype(F32) for a in at]
        flat[pl.ds(pl.multiple_of(8 * i, 8), 8), :] = jnp.concatenate(v, axis=0)


def kernel(
    q, scales, place, tokens, experts, replica, route,
    w_new, scale_out, hidden_out, load_out,
    place_tx, place_rx, place_sm, meta_tx, meta_rx,
    r0, r1, r2, r3, y0, y1, y2, y3, s0, s1, s2, s3,
    big, tx, mid, rx, xm, acc, back_tx, back_mid, back_rx, qbuf, grow, placed_t,
    sem_place, sem_spread, sem_meta, sem_1s, sem_1r, sem_2s, sem_2r, sem_3s, sem_3r, sem_own1, sem_own3,
    sem_tok, sem_tok2, sem_ret, sem_ret2, sem_local, sem_q,
):
    g = lax.axis_index("group")
    d = lax.axis_index("dev")
    z, x = d // 4, d % 4
    me = g * ND + d

    def peer(o):
        return lax.rem(z + o[0], 4) * 4 + lax.rem(x + o[1], 4)

    def remote(src, dst, ssem, rsem, dev):
        return pltpu.make_async_remote_copy(
            src_ref=src, dst_ref=dst, send_sem=ssem, recv_sem=rsem,
            device_id=dev, device_id_type=MESH,
        )

    def across(i):
        return lax.rem(g + i, NG)

    barrier = pltpu.get_barrier_semaphore()

    for o in ORDER:
        pl.semaphore_signal(barrier, inc=1, device_id=(g, peer(o)), device_id_type=MESH)
    for i in range(1, NG):
        pl.semaphore_signal(barrier, inc=1, device_id=(across(i), d), device_id_type=MESH)

    place_tx[...] = jnp.full((1, 128), place[0], I32)
    place_rx[me] = jnp.full((1, 128), place[0], I32)
    widen = (iota((KT, 128), 0) == iota((KT, 128), 1)).astype(BF)
    spread = [jnp.dot(scales[m], widen, preferred_element_type=F32) for m in range(HOLD)]
    meta_tx[...] = jnp.concatenate(spread, axis=0).astype(BF)

    pl.semaphore_wait(barrier, ND - 1 + NG - 1)

    for o in ORDER:
        remote(place_tx, place_rx.at[me], sem_place.at[0], sem_place.at[1], (g, peer(o))).start()
    for o in ORDER:
        remote(meta_tx, meta_rx.at[d], sem_meta.at[0], sem_meta.at[1], (g, peer(o))).start()
    meta_own = pltpu.make_async_copy(meta_tx, meta_rx.at[d], sem_local.at[0])
    meta_own.start()

    relays = (r0, r1, r2, r3)
    swaps = (y0, y1, y2, y3)
    sends = (s0, s1, s2, s3)

    def place_of(axis):
        return (z, x) if axis == 0 else (x, z)

    def dev_of(axis, u, v):
        return u * 4 + v if axis == 0 else v * 4 + u

    def mod4(i):
        return lax.rem(i + 8, 4)

    def piece_rows(c, first, n):
        return pl.ds(pl.multiple_of(c * PIECE + first, SUB), n)

    def piece_cols(r, f):
        return pl.ds(pl.multiple_of(r * 256 + f * 128, 128), 128)

    KINDS = ((0, 0, 0, 1), (0, 1, -1, 0), (1, 0, 1, 0), (-1, 1, -2, 1))
    FIRST = ((1, 0), (3, 0), (0, 2), (0, 3), (1, 1), (3, 1), (1, 2), (3, 3), (3, 2), (1, 3), (2, 0), (2, 2), (2, 1), (2, 3))

    def supply(k, dv, kind, at, n):
        f, _, base, rows, axis = CHUNKS[k]
        u, v = place_of(axis)
        step, role, piece, line = KINDS[kind]
        r = mod4(v + dv)
        src = q.at[:, piece_rows(mod4(u + piece), base + at, n), piece_cols(r, f)]
        entry = role * 16 + (line * 4 + v) * 2
        dst = relays[k].at[pl.ds(entry, 2), pl.ds(pl.multiple_of(at, SUB), n)]
        return src, dst, (g, dev_of(axis, mod4(u + step), r))

    def supply_sends(ks, at):
        for dv, kind in FIRST:
            for k in ks:
                src, dst, dev = supply(k, dv, kind, at, SUB)
                remote(src, dst, sem_1s.at[k], sem_1r.at[k], dev).start()

    def supply_own(k):
        cps = []
        for kind in range(2):
            src, dst, _ = supply(k, 0, kind, 0, CHUNKS[k][3])
            cps.append(pltpu.make_async_copy(src, dst, sem_own1.at[k, kind]))
        return cps

    def supply_steps(pair, lo, hi):
        @pl.loop(lo, hi)
        def _(i):
            supply_sends(pair, i * SUB)

    supply_steps((0, 1), 0, EARLY)
    own = [supply_own(k) for k in range(4)]
    for cps in own:
        for cp in cps:
            cp.start()

    def q_copy(i):
        return pltpu.make_async_copy(
            q.at[i // (D // QROWS), pl.ds(pl.multiple_of(lax.rem(i, D // QROWS) * QROWS, QROWS), QROWS)],
            qbuf.at[lax.rem(i, 2)], sem_q.at[lax.rem(i, 2)],
        )

    q_copy(0).start()

    def to_row(a):
        rep = (iota((ROWS, PAIRS), 1) // TOPK == iota((ROWS, PAIRS), 0)).astype(BF)
        wide = jnp.dot(a[...].astype(F32).astype(BF), rep, preferred_element_type=F32)
        mine = lax.rem(iota((TOPK, PAIRS), 1), TOPK) == iota((TOPK, PAIRS), 0)
        return jnp.sum(jnp.where(mine, wide, 0.0), axis=0, keepdims=True)

    def to_col(row):
        return jnp.broadcast_to(row, (PAIRS, PAIRS)).T

    expert_row = to_row(experts)
    replica_row = to_row(replica)
    weight_col = to_col(to_row(route) * (1.0 / 16.0))

    def wait_recv_all(ref, sem):
        pltpu.make_async_copy(ref, ref, sem).wait()

    group_rows = pl.ds(pl.multiple_of(g * ND, ND), ND)
    wait_recv_all(place_rx.at[pl.ds(0, ND - 1)], sem_place.at[1])
    for i in range(1, NG):
        remote(
            place_rx.at[group_rows], place_rx.at[group_rows], sem_spread.at[0], sem_spread.at[1], (across(i), d)
        ).start()
    sm = pltpu.make_async_copy(place_rx.at[group_rows], place_sm, sem_local.at[3])
    sm.start()
    wait_recv_all(place_rx.at[pl.ds(0, ND * (NG - 1))], sem_spread.at[1])

    hold_of = place_rx[...].reshape(N, 128).astype(F32)
    match = hold_of == expert_row
    dev_ids = iota((N, PAIRS), 0).astype(F32)
    holder = jnp.sum(jnp.where(match, dev_ids, 0.0), axis=0, keepdims=True)
    found = jnp.sum(jnp.where(match, 1.0, 0.0), axis=0, keepdims=True)
    use_copy = (replica_row > 0.5) & (found > 0.5)
    home = jnp.floor(expert_row * 0.5)
    target = jnp.where(use_copy, holder, home)
    slot = jnp.where(use_copy, float(HOLD), expert_row - 2.0 * home)
    target_col = to_col(target)
    slot_col = to_col(slot)
    earlier = (target_col == target) & (iota((PAIRS, PAIRS), 0) < iota((PAIRS, PAIRS), 1))
    position = jnp.sum(jnp.where(earlier, 1.0, 0.0), axis=0, keepdims=True)
    cell = jnp.where(position < CAP, target * CAP + position, -1.0)
    placed = jnp.where(iota((CELLS, PAIRS), 0).astype(F32) == cell, 1.0, 0.0)
    cell_col = jnp.concatenate([to_col(cell)] * 2, axis=1)
    placed_t[...] = jnp.where(iota((PAIRS, CELLS), 1).astype(F32) == cell_col, 1.0, 0.0).astype(BF)
    placed = placed.astype(BF)
    to_rows = (iota((PAIRS, ROWS), 0) // TOPK == iota((PAIRS, ROWS), 1)).astype(BF)
    row_pick = jnp.dot(placed, to_rows, preferred_element_type=F32).astype(BF)

    @pl.loop(0, D // 512)
    def _(i):
        cols = pl.ds(pl.multiple_of(i * 512, 512), 512)
        big[:, cols] = jnp.dot(row_pick, tokens[:, cols], preferred_element_type=F32)

    big[:, D:] = jnp.dot(placed, (slot_col + 1.0).astype(BF), preferred_element_type=F32) - 1.0

    unpack_rows(big, tx)

    for i in range(1, NG):
        t = across(i)
        remote(
            tx.at[pl.ds(pl.multiple_of(t * ND, ND), ND)], mid.at[g], sem_tok.at[0], sem_tok.at[1], (t, d)
        ).start()
    mid_own = pltpu.make_async_copy(tx.at[group_rows], mid.at[g], sem_local.at[8])
    mid_own.start()
    supply_steps((0, 1), EARLY, 6)
    supply_steps((0,), 6, 8)
    mid_own.wait()
    wait_recv_all(mid.at[pl.ds(0, NG - 1)], sem_tok.at[1])
    for o in ORDER:
        p = peer(o)
        remote(mid.at[:, p], rx.at[d], sem_tok2.at[0], sem_tok2.at[1], (g, p)).start()
    tok_own = pltpu.make_async_copy(mid.at[:, d], rx.at[d], sem_local.at[4])
    tok_own.start()
    supply_steps((2, 3), 0, 6)
    supply_steps((2,), 6, 8)


    def wanted(axis, u, v):
        w = place_sm[dev_of(axis, u, v), 0, 0]
        s = lax.rem(w // HOLD, ND)
        su, sv = (s // 4, lax.rem(s, 4)) if axis == 0 else (lax.rem(s, 4), s // 4)
        return su, sv, lax.rem(w, HOLD)

    def entry_of(role, u, want):
        su, sv, m = want
        line = (su == u).astype(I32) if role == 0 else (su != u).astype(I32)
        return role * 16 + (line * 4 + sv) * 2 + m

    def trade_pick(k):
        _, _, _, rows, axis = CHUNKS[k]
        u, v = place_of(axis)
        for cp in own[k]:
            cp.wait()
        wait_recv_all(relays[k].at[pl.ds(0, 28)], sem_1r.at[k])
        for role in range(2):
            @pl.loop(0, 8)
            def _(j, role=role):
                line = mod4(u + (1 if role == 0 else -2) + j // 4)
                want = wanted(axis, line, lax.rem(j, 4))
                sends[k][role * 8 + j] = relays[k][entry_of(role, u, want)]

    def trade(pair):
        for k in pair:
            trade_pick(k)

        @pl.loop(0, 8)
        def _(j):
            for role in range(2):
                for k in pair:
                    axis = CHUNKS[k][4]
                    u, v = place_of(axis)
                    to = dev_of(axis, mod4(u + (1 if role == 0 else -1)), v)
                    remote(
                        sends[k].at[role * 8 + j], swaps[k].at[(1 - role) * 8 + j],
                        sem_2s.at[k], sem_2r.at[k], (g, to),
                    ).start()

    def landing(k, role):
        f, _, base, rows, axis = CHUNKS[k]
        u, v = place_of(axis)
        c = u if role == 0 else mod4(u - 1)
        return w_new.at[piece_rows(c, base, rows), piece_cols(v, f)]

    LAST = (
        (1, 0, 1), (3, 0, 1), (0, 0, 0), (0, 1, 1), (1, 1, 0), (3, 1, 0), (1, 0, 0), (3, 1, 1),
        (3, 0, 0), (1, 1, 1), (2, 0, 1), (2, 1, 1), (2, 1, 0), (2, 0, 0),
    )

    def own_slot(axis, role):
        _, v = place_of(axis)
        return role * 8 + (4 if role == 0 else 0) + v

    def deliver_pick(k):
        _, _, _, rows, axis = CHUNKS[k]
        u, v = place_of(axis)
        wait_recv_all(swaps[k], sem_2r.at[k])
        wait_recv_all(sends[k], sem_2s.at[k])
        for role in range(2):
            @pl.loop(0, 8)
            def _(j, role=role):
                line = mod4(u + (-1 if role == 0 else 0) + j // 4)
                want = wanted(axis, line, lax.rem(j, 4))
                near = (want[0] == u) | (want[0] == mod4(u + (-1 if role == 0 else 1)))
                mine = relays[k][entry_of(role, u, want)]
                other = swaps[k][role * 8 + j]
                sends[k][role * 8 + j] = jnp.where(near, mine, other)
        for role in range(2):
            own_part(k, role).start()

    def deliver(pair):
        for k in pair:
            deliver_pick(k)
        for i, (dv, role, line) in enumerate(LAST):
            for k in pair:
                axis = CHUNKS[k][4]
                u, v = place_of(axis)
                r = mod4(v + dv)
                to = dev_of(axis, mod4(u + line - (1 if role == 0 else 0)), r)
                remote(
                    sends[k].at[role * 8 + line * 4 + r], landing(k, role), sem_3s.at[k], sem_3r.at[k, i], (g, to)
                ).start()

    def own_part(k, role):
        return pltpu.make_async_copy(
            sends[k].at[own_slot(CHUNKS[k][4], role)], landing(k, role), sem_own3.at[k, role]
        )

    sm.wait()

    meta_own.wait()
    wait_recv_all(meta_rx.at[pl.ds(0, ND - 1)], sem_meta.at[1])
    mine_w = place[0]
    got = meta_rx[lax.rem(mine_w // HOLD, ND)]
    slot_m = lax.rem(mine_w, HOLD)
    got_wide = got.astype(F32)
    mine_scales = jnp.where(slot_m == 0, got_wide[0:8], got_wide[8:16])
    scale_out[...] = mine_scales[:, 0:KT].astype(BF)

    def grow_scales(block, m, f):
        tiles = 2 * (iota((128, HALF), 1) // TILE) + f
        sel = (iota((128, HALF), 0) == tiles + 8 * m).astype(BF)
        tall = jnp.concatenate([block.astype(F32), jnp.zeros((112, 128), F32)], axis=0).T
        return jnp.dot(tall[0:32].astype(BF), sel, preferred_element_type=F32).reshape(32, 1, HALF)

    for f in range(2):
        for m in range(HOLD):
            grow[m, f] = grow_scales(meta_tx[...], m, f)
        grow[HOLD, f] = grow_scales(got, slot_m, f)

    tok_own.wait()
    wait_recv_all(rx.at[pl.ds(0, ND - 1)], sem_tok2.at[1])

    pack_rows(rx, big, True)

    code = big[:, D:]
    load_row = jnp.zeros((1, 128), F32)
    for s in range(HOLD + 1):
        count = jnp.sum(jnp.where(code == float(s), 1.0, 0.0), axis=0, keepdims=True)
        load_row = jnp.where(iota((1, 128), 1) == s, count, load_row)
    load_out[...] = load_row[:, 0 : HOLD + 1].astype(I32)

    for s in range(HOLD + 1):
        @pl.loop(0, KT)
        def _(k, s=s):
            cols = pl.ds(pl.multiple_of(k * TILE, TILE), TILE)
            xm[s, :, cols] = jnp.where(code == float(s), big[:, cols], 0.0).astype(BF)

    acc[...] = jnp.zeros((2, CELLS, HALF), F32)
    n_q = HOLD * (D // QROWS)

    @pl.loop(0, n_q)
    def _(i):
        @pl.when(i + 1 < n_q)
        def _():
            q_copy(i + 1).start()
        q_copy(i).wait()
        m = i // (D // QROWS)
        tile0 = lax.rem(i, D // QROWS) * (QROWS // TILE)
        xs = xm[m, :, pl.ds(pl.multiple_of(tile0 * TILE, TILE), QROWS)]
        for f in range(2):
            cols = [qbuf[lax.rem(i, 2), :, 256 * r + 128 * f : 256 * r + 128 * f + 128] for r in range(4)]
            w = jnp.concatenate(cols, axis=1).astype(F32).reshape(QROWS // TILE, TILE, HALF)
            w = (w * grow[m, f, pl.ds(tile0, QROWS // TILE)]).astype(BF).reshape(QROWS, HALF)
            acc[f] += jnp.dot(xs, w, preferred_element_type=F32)

    trade((0, 1))
    trade((2, 3))
    deliver((0, 1))
    deliver((2, 3))

    def serve_part(k, c, r):
        f, _, base, rows, _ = CHUNKS[k]
        at = piece_rows(c, base, rows)
        tiles = pl.ds(c * (PIECE // TILE) + base // TILE, rows // TILE)
        cols = pl.ds(pl.multiple_of(r * 128, 128), 128)
        w = w_new[at, piece_cols(r, f)].astype(F32).reshape(rows // TILE, TILE, 128)
        w = (w * grow[HOLD, f, tiles, :, cols]).astype(BF).reshape(rows, 128)
        acc[f, :, cols] += jnp.dot(xm[HOLD, :, at], w, preferred_element_type=F32)

    def serve_own(pair):
        for k in pair:
            u, v = place_of(CHUNKS[k][4])
            for role in range(2):
                own_part(k, role).wait()
                serve_part(k, u if role == 0 else mod4(u - 1), v)

    def serve(pair, lo, hi):
        for i, (dv, role, line) in list(enumerate(LAST))[lo:hi]:
            for k in pair:
                u, v = place_of(CHUNKS[k][4])
                got = w_new.at[pl.ds(0, CHUNKS[k][3]), pl.ds(0, 128)]
                pltpu.make_async_copy(got, got, sem_3r.at[k, i]).wait()
                c = mod4(u - line + (1 if role == 0 else -1))
                serve_part(k, c, mod4(v - dv))

    def back_rows(p):
        return pl.ds(pl.multiple_of(p * NG, NG), NG)

    def finish(f):
        v = acc[f]
        acc[f] = v / (1.0 + jnp.exp(-v))
        unpack_rows(acc.at[f], back_tx.at[f])
        for o in ORDER:
            p = peer(o)
            remote(
                back_tx.at[f, back_rows(p)], back_mid.at[f, :, d], sem_ret.at[f, 0], sem_ret.at[f, 1], (g, peer(o))
            ).start()
        back_copy(f).start()

    def back_copy(f):
        return pltpu.make_async_copy(back_tx.at[f, back_rows(d)], back_mid.at[f, :, d], sem_local.at[5 + f])

    def back_own(f):
        return pltpu.make_async_copy(back_mid.at[f, g], back_rx.at[f, group_rows], sem_local.at[9 + f])

    def back_across(f):
        back_copy(f).wait()
        wait_recv_all(back_mid.at[f, :, pl.ds(0, ND - 1)], sem_ret.at[f, 1])
        for i in range(1, NG):
            t = across(i)
            remote(
                back_mid.at[f, t], back_rx.at[f, group_rows], sem_ret2.at[f, 0], sem_ret2.at[f, 1], (t, d)
            ).start()
        back_own(f).start()

    def arrive(f):
        back_own(f).wait()
        wait_recv_all(back_rx.at[f, pl.ds(0, ND * (NG - 1))], sem_ret2.at[f, 1])
        pack_rows(back_rx.at[f], acc.at[f])
        part = jnp.dot(placed_t[...], acc[f].astype(BF), preferred_element_type=F32)
        part = (part * weight_col[:, 0:1]).astype(BF)
        for r in range(4):
            hidden_out[:, 256 * r + 128 * f : 256 * r + 128 * f + 128] = part[:, 128 * r : 128 * r + 128]

    serve_own((0, 1))
    serve((0, 1), 0, 14)
    finish(0)
    serve_own((2, 3))
    serve((2, 3), 0, 14)
    finish(1)
    back_across(0)
    arrive(0)
    back_across(1)
    arrive(1)

    wait_recv_all(place_rx.at[pl.ds(0, ND - 1)], sem_place.at[0])
    wait_recv_all(place_rx.at[pl.ds(0, ND * (NG - 1))], sem_spread.at[0])
    wait_recv_all(meta_rx.at[pl.ds(0, ND - 1)], sem_meta.at[0])
    for k in range(4):
        wait_recv_all(relays[k].at[pl.ds(0, 28)], sem_1s.at[k])
        wait_recv_all(sends[k].at[pl.ds(0, 14)], sem_3s.at[k])
    wait_recv_all(mid.at[pl.ds(0, NG - 1)], sem_tok.at[0])
    wait_recv_all(rx.at[pl.ds(0, ND - 1)], sem_tok2.at[0])
    for f in range(2):
        wait_recv_all(back_mid.at[f, :, pl.ds(0, ND - 1)], sem_ret.at[f, 0])
        wait_recv_all(back_rx.at[f, pl.ds(0, ND * (NG - 1))], sem_ret2.at[f, 0])


def store(w, scale, hidden, load, w_out, scale_out, hidden_out, load_out, sems):
    n = 4
    part = D // n
    copies = [
        pltpu.make_async_copy(w.at[pl.ds(i * part, part)], w_out.at[pl.ds(i * part, part)], sems.at[i]) for i in range(n)
    ]
    for i, (a, b) in enumerate(((scale, scale_out), (hidden, hidden_out), (load, load_out))):
        copies.append(pltpu.make_async_copy(a, b, sems.at[n + i]))
    for c in copies:
        c.start()
    for c in copies:
        c.wait()


def per_device(primary_q, primary_scales, new_place, tokens, experts, replica, route_num):
    vmem = pl.BlockSpec(memory_space=pltpu.VMEM)
    anywhere = pl.BlockSpec(memory_space=pl.ANY)
    dma = pltpu.SemaphoreType.DMA
    scratch = [
        pltpu.VMEM((1, 128), I32),
        pltpu.VMEM((N, 1, 128), I32),
        pltpu.SMEM((ND, 1, 128), I32),
        pltpu.VMEM((16, 128), BF),
        pltpu.VMEM((ND, 16, 128), BF),
        *[pltpu.VMEM((32, c[3], 128), BF) for c in CHUNKS],
        *[pltpu.VMEM((16, c[3], 128), BF) for c in CHUNKS],
        *[pltpu.VMEM((16, c[3], 128), BF) for c in CHUNKS],
        pltpu.VMEM((CELLS, WIDE), F32),
        pltpu.VMEM((N, CAP, WIDE), BF),
        pltpu.VMEM((NG, ND, CAP, WIDE), BF),
        pltpu.VMEM((ND, NG, CAP, WIDE), BF),
        pltpu.VMEM((HOLD + 1, CELLS, D), BF),
        pltpu.VMEM((2, CELLS, HALF), F32),
        pltpu.VMEM((2, N, CAP, HALF), BF),
        pltpu.VMEM((2, NG, ND, CAP, HALF), BF),
        pltpu.VMEM((2, N, CAP, HALF), BF),
        pltpu.VMEM((2, QROWS, FF), BF),
        pltpu.VMEM((HOLD + 1, 2, 32, 1, HALF), F32),
        pltpu.VMEM((PAIRS, CELLS), BF),
        dma((2,)), dma((2,)), dma((2,)), dma((4,)), dma((4,)), dma((4,)), dma((4,)), dma((4,)), dma((4, 14)),
        dma((4, 2)), dma((4, 2)),
        dma((2,)), dma((2,)), dma((2, 2)), dma((2, 2)), dma((11,)), dma((2,)),
    ]
    new_weights, scale_tile, hidden, load = pl.pallas_call(
        kernel,
        out_shape=(
            pltpu.VMEM((D, FF), BF),
            pltpu.VMEM((8, KT), BF),
            pltpu.VMEM((PAIRS, FF), BF),
            pltpu.VMEM((1, HOLD + 1), I32),
        ),
        in_specs=[
            anywhere, vmem, pl.BlockSpec(memory_space=pltpu.SMEM), vmem, vmem, vmem, vmem,
        ],
        out_specs=(vmem, vmem, vmem, vmem),
        scratch_shapes=scratch,
        compiler_params=pltpu.CompilerParams(
            collective_id=0, has_side_effects=True, vmem_limit_bytes=56000 * 1024
        ),
    )(
        primary_q, primary_scales.transpose(0, 2, 1), new_place, tokens,
        experts.T, replica.T, route_num.T,
    )
    results = [
        pltpu.with_memory_space_constraint(a, pltpu.VMEM) for a in (new_weights, scale_tile, hidden, load)
    ]
    new_weights, scale_tile, hidden, load = pl.pallas_call(
        store,
        out_shape=(
            jax.ShapeDtypeStruct((D, FF), BF),
            jax.ShapeDtypeStruct((8, KT), BF),
            jax.ShapeDtypeStruct((PAIRS, FF), BF),
            jax.ShapeDtypeStruct((1, HOLD + 1), I32),
        ),
        in_specs=[vmem] * 4,
        out_specs=(anywhere,) * 4,
        scratch_shapes=[dma((7,))],
        compiler_params=pltpu.CompilerParams(vmem_limit_bytes=1024 * 1024),
    )(*results)
    return (
        new_weights.reshape(1, D, FF),
        scale_tile.T.reshape(1, KT, 8),
        hidden.reshape(ROWS, TOPK, FF),
        load,
    )


def solution(mesh):
    both = ("group", "dev")
    return jax.shard_map(
        per_device,
        mesh=mesh,
        in_specs=(
            P(both, None, None), P(both, None, None), P(both), P(both, None),
            P(both, None), P(both, None), P(both, None),
        ),
        out_specs=(P(both, None, None), P(both, None, None), P(both, None, None), P(both, None)),
        check_vma=False,
    )
```

```python
import jax
import jax.numpy as jnp
from jax import lax
from jax.experimental import pallas as pl
from jax.experimental.pallas import tpu as pltpu
from jax.sharding import PartitionSpec as P

D = 3584
FF = 1024
TILE = 128
CAP = 2
HOLD = 2
NG = 8
ND = 16
N = NG * ND
ROWS = 16
TOPK = 8
PAIRS = ROWS * TOPK
CELLS = N * CAP
KT = D // TILE
WIDE = D + 128
BF = jnp.bfloat16
F32 = jnp.float32
I32 = jnp.int32
MESH = pl.DeviceIdType.MESH

ORDER = (
    (0, 1), (0, 3), (1, 0), (3, 0), (1, 1), (3, 3), (1, 3), (3, 1),
    (0, 2), (2, 0), (2, 2), (1, 2), (3, 2), (2, 1), (2, 3),
)
CHUNKS = ((0, 0, 0, 512, 0), (0, 1, 512, 384, 1), (1, 0, 0, 512, 1), (1, 1, 512, 384, 0))
PIECE = 896
HALF = 512
SUB = 64
EARLY = 4
QROWS = 512


def iota(shape, dim):
    return lax.broadcasted_iota(I32, shape, dim)


def unpack_rows(flat, blocks):
    @pl.loop(0, CELLS // 8)
    def _(i):
        v = flat[pl.ds(pl.multiple_of(8 * i, 8), 8), :]
        for j in range(4):
            blocks[4 * i + j] = v[2 * j : 2 * j + 2].astype(BF)


def unpack_part(flat, blocks, p):
    for h in range(2):
        v = flat[pl.ds(pl.multiple_of(16 * p + 8 * h, 8), 8), :]
        for j in range(4):
            blocks[8 * p + 4 * h + j] = v[2 * j : 2 * j + 2].astype(BF)


def pack_rows(blocks, flat, nested=False):
    @pl.loop(0, CELLS // 8)
    def _(i):
        at = [(i // 2, lax.rem(i, 2) * 4 + j) if nested else (4 * i + j,) for j in range(4)]
        v = [blocks[a].astype(F32) for a in at]
        flat[pl.ds(pl.multiple_of(8 * i, 8), 8), :] = jnp.concatenate(v, axis=0)


def kernel(
    q, scales, place, tokens, experts, replica, route,
    w_new, scale_out, hidden_out, load_out,
    place_tx, place_rx, place_sm, meta_tx, meta_rx,
    r0, r1, r2, r3, y0, y1, y2, y3, s0, s1, s2, s3,
    big, tx, mid, rx, xm, acc, back_tx, back_mid, back_rx, qbuf, grow, placed_t,
    sem_place, sem_spread, sem_meta, sem_1s, sem_1r, sem_2s, sem_2r, sem_3s, sem_3r, sem_own1, sem_own3,
    sem_tok, sem_tok2, sem_ret, sem_ret2, sem_local, sem_q,
):
    g = lax.axis_index("group")
    d = lax.axis_index("dev")
    z, x = d // 4, d % 4
    me = g * ND + d

    def peer(o):
        return lax.rem(z + o[0], 4) * 4 + lax.rem(x + o[1], 4)

    def remote(src, dst, ssem, rsem, dev):
        return pltpu.make_async_remote_copy(
            src_ref=src, dst_ref=dst, send_sem=ssem, recv_sem=rsem,
            device_id=dev, device_id_type=MESH,
        )

    def across(i):
        return lax.rem(g + i, NG)

    barrier = pltpu.get_barrier_semaphore()

    for o in ORDER:
        pl.semaphore_signal(barrier, inc=1, device_id=(g, peer(o)), device_id_type=MESH)
    for i in range(1, NG):
        pl.semaphore_signal(barrier, inc=1, device_id=(across(i), d), device_id_type=MESH)

    place_tx[...] = jnp.full((1, 128), place[0], I32)
    place_rx[me] = jnp.full((1, 128), place[0], I32)
    widen = (iota((KT, 128), 0) == iota((KT, 128), 1)).astype(BF)
    spread = [jnp.dot(scales[m], widen, preferred_element_type=F32) for m in range(HOLD)]
    meta_tx[...] = jnp.concatenate(spread, axis=0).astype(BF)

    pl.semaphore_wait(barrier, ND - 1 + NG - 1)

    for o in ORDER:
        remote(place_tx, place_rx.at[me], sem_place.at[0], sem_place.at[1], (g, peer(o))).start()
    for o in ORDER:
        remote(meta_tx, meta_rx.at[d], sem_meta.at[0], sem_meta.at[1], (g, peer(o))).start()
    meta_own = pltpu.make_async_copy(meta_tx, meta_rx.at[d], sem_local.at[0])
    meta_own.start()

    relays = (r0, r1, r2, r3)
    swaps = (y0, y1, y2, y3)
    sends = (s0, s1, s2, s3)

    def place_of(axis):
        return (z, x) if axis == 0 else (x, z)

    def dev_of(axis, u, v):
        return u * 4 + v if axis == 0 else v * 4 + u

    def mod4(i):
        return lax.rem(i + 8, 4)

    def piece_rows(c, first, n):
        return pl.ds(pl.multiple_of(c * PIECE + first, SUB), n)

    def piece_cols(r, f):
        return pl.ds(pl.multiple_of(r * 256 + f * 128, 128), 128)

    KINDS = ((0, 0, 0, 1), (0, 1, -1, 0), (1, 0, 1, 0), (-1, 1, -2, 1))
    FIRST = ((1, 0), (3, 0), (0, 2), (0, 3), (1, 1), (3, 1), (1, 2), (3, 3), (3, 2), (1, 3), (2, 0), (2, 2), (2, 1), (2, 3))

    def supply(k, dv, kind, at, n):
        f, _, base, rows, axis = CHUNKS[k]
        u, v = place_of(axis)
        step, role, piece, line = KINDS[kind]
        r = mod4(v + dv)
        src = q.at[:, piece_rows(mod4(u + piece), base + at, n), piece_cols(r, f)]
        entry = role * 16 + (line * 4 + v) * 2
        dst = relays[k].at[pl.ds(entry, 2), pl.ds(pl.multiple_of(at, SUB), n)]
        return src, dst, (g, dev_of(axis, mod4(u + step), r))

    def supply_sends(ks, at):
        for dv, kind in FIRST:
            for k in ks:
                src, dst, dev = supply(k, dv, kind, at, SUB)
                remote(src, dst, sem_1s.at[k], sem_1r.at[k], dev).start()

    def supply_own(k):
        cps = []
        for kind in range(2):
            src, dst, _ = supply(k, 0, kind, 0, CHUNKS[k][3])
            cps.append(pltpu.make_async_copy(src, dst, sem_own1.at[k, kind]))
        return cps

    def supply_steps(pair, lo, hi):
        @pl.loop(lo, hi)
        def _(i):
            supply_sends(pair, i * SUB)

    supply_steps((0, 1), 0, EARLY)
    own = [supply_own(k) for k in range(4)]
    for cps in own:
        for cp in cps:
            cp.start()

    def q_copy(i):
        return pltpu.make_async_copy(
            q.at[i // (D // QROWS), pl.ds(pl.multiple_of(lax.rem(i, D // QROWS) * QROWS, QROWS), QROWS)],
            qbuf.at[lax.rem(i, 2)], sem_q.at[lax.rem(i, 2)],
        )

    q_copy(0).start()

    def to_row(a):
        rep = (iota((ROWS, PAIRS), 1) // TOPK == iota((ROWS, PAIRS), 0)).astype(BF)
        wide = jnp.dot(a[...].astype(F32).astype(BF), rep, preferred_element_type=F32)
        mine = lax.rem(iota((TOPK, PAIRS), 1), TOPK) == iota((TOPK, PAIRS), 0)
        return jnp.sum(jnp.where(mine, wide, 0.0), axis=0, keepdims=True)

    def to_col(row):
        return jnp.broadcast_to(row, (PAIRS, PAIRS)).T

    expert_row = to_row(experts)
    replica_row = to_row(replica)
    weight_col = to_col(to_row(route) * (1.0 / 16.0))

    def wait_recv_all(ref, sem):
        pltpu.make_async_copy(ref, ref, sem).wait()

    group_rows = pl.ds(pl.multiple_of(g * ND, ND), ND)
    wait_recv_all(place_rx.at[pl.ds(0, ND - 1)], sem_place.at[1])
    for i in range(1, NG):
        remote(
            place_rx.at[group_rows], place_rx.at[group_rows], sem_spread.at[0], sem_spread.at[1], (across(i), d)
        ).start()
    sm = pltpu.make_async_copy(place_rx.at[group_rows], place_sm, sem_local.at[3])
    sm.start()
    wait_recv_all(place_rx.at[pl.ds(0, ND * (NG - 1))], sem_spread.at[1])

    hold_of = place_rx[...].reshape(N, 128).astype(F32)
    match = hold_of == expert_row
    dev_ids = iota((N, PAIRS), 0).astype(F32)
    holder = jnp.sum(jnp.where(match, dev_ids, 0.0), axis=0, keepdims=True)
    found = jnp.sum(jnp.where(match, 1.0, 0.0), axis=0, keepdims=True)
    use_copy = (replica_row > 0.5) & (found > 0.5)
    home = jnp.floor(expert_row * 0.5)
    target = jnp.where(use_copy, holder, home)
    slot = jnp.where(use_copy, float(HOLD), expert_row - 2.0 * home)
    target_col = to_col(target)
    slot_col = to_col(slot)
    earlier = (target_col == target) & (iota((PAIRS, PAIRS), 0) < iota((PAIRS, PAIRS), 1))
    position = jnp.sum(jnp.where(earlier, 1.0, 0.0), axis=0, keepdims=True)
    cell = jnp.where(position < CAP, target * CAP + position, -1.0)
    placed = jnp.where(iota((CELLS, PAIRS), 0).astype(F32) == cell, 1.0, 0.0)
    cell_col = jnp.concatenate([to_col(cell)] * 2, axis=1)
    placed_t[...] = jnp.where(iota((PAIRS, CELLS), 1).astype(F32) == cell_col, 1.0, 0.0).astype(BF)
    placed = placed.astype(BF)
    to_rows = (iota((PAIRS, ROWS), 0) // TOPK == iota((PAIRS, ROWS), 1)).astype(BF)
    row_pick = jnp.dot(placed, to_rows, preferred_element_type=F32).astype(BF)

    @pl.loop(0, D // 512)
    def _(i):
        cols = pl.ds(pl.multiple_of(i * 512, 512), 512)
        big[:, cols] = jnp.dot(row_pick, tokens[:, cols], preferred_element_type=F32)

    big[:, D:] = jnp.dot(placed, (slot_col + 1.0).astype(BF), preferred_element_type=F32) - 1.0

    unpack_rows(big, tx)

    for i in range(1, NG):
        t = across(i)
        remote(
            tx.at[pl.ds(pl.multiple_of(t * ND, ND), ND)], mid.at[g], sem_tok.at[0], sem_tok.at[1], (t, d)
        ).start()
    mid_own = pltpu.make_async_copy(tx.at[group_rows], mid.at[g], sem_local.at[8])
    mid_own.start()
    supply_steps((0, 1), EARLY, 6)
    supply_steps((0,), 6, 8)
    mid_own.wait()
    wait_recv_all(mid.at[pl.ds(0, NG - 1)], sem_tok.at[1])
    for o in ORDER:
        p = peer(o)
        remote(mid.at[:, p], rx.at[d], sem_tok2.at[0], sem_tok2.at[1], (g, p)).start()
    tok_own = pltpu.make_async_copy(mid.at[:, d], rx.at[d], sem_local.at[4])
    tok_own.start()
    supply_steps((2, 3), 0, 6)
    supply_steps((2,), 6, 8)


    def wanted(axis, u, v):
        w = place_sm[dev_of(axis, u, v), 0, 0]
        s = lax.rem(w // HOLD, ND)
        su, sv = (s // 4, lax.rem(s, 4)) if axis == 0 else (lax.rem(s, 4), s // 4)
        return su, sv, lax.rem(w, HOLD)

    def entry_of(role, u, want):
        su, sv, m = want
        line = (su == u).astype(I32) if role == 0 else (su != u).astype(I32)
        return role * 16 + (line * 4 + sv) * 2 + m

    def trade_pick(k):
        _, _, _, rows, axis = CHUNKS[k]
        u, v = place_of(axis)
        for cp in own[k]:
            cp.wait()
        wait_recv_all(relays[k].at[pl.ds(0, 28)], sem_1r.at[k])
        for role in range(2):
            @pl.loop(0, 8)
            def _(j, role=role):
                line = mod4(u + (1 if role == 0 else -2) + j // 4)
                want = wanted(axis, line, lax.rem(j, 4))
                sends[k][role * 8 + j] = relays[k][entry_of(role, u, want)]

    def trade(pair):
        for k in pair:
            trade_pick(k)

        @pl.loop(0, 8)
        def _(j):
            for role in range(2):
                for k in pair:
                    axis = CHUNKS[k][4]
                    u, v = place_of(axis)
                    to = dev_of(axis, mod4(u + (1 if role == 0 else -1)), v)
                    remote(
                        sends[k].at[role * 8 + j], swaps[k].at[(1 - role) * 8 + j],
                        sem_2s.at[k], sem_2r.at[k], (g, to),
                    ).start()

    def landing(k, role):
        f, _, base, rows, axis = CHUNKS[k]
        u, v = place_of(axis)
        c = u if role == 0 else mod4(u - 1)
        return w_new.at[piece_rows(c, base, rows), piece_cols(v, f)]

    LAST = (
        (1, 0, 1), (3, 0, 1), (0, 0, 0), (0, 1, 1), (1, 1, 0), (3, 1, 0), (1, 0, 0), (3, 1, 1),
        (3, 0, 0), (1, 1, 1), (2, 0, 1), (2, 1, 1), (2, 1, 0), (2, 0, 0),
    )

    def own_slot(axis, role):
        _, v = place_of(axis)
        return role * 8 + (4 if role == 0 else 0) + v

    def deliver_pick(k):
        _, _, _, rows, axis = CHUNKS[k]
        u, v = place_of(axis)
        wait_recv_all(swaps[k], sem_2r.at[k])
        wait_recv_all(sends[k], sem_2s.at[k])
        for role in range(2):
            @pl.loop(0, 8)
            def _(j, role=role):
                line = mod4(u + (-1 if role == 0 else 0) + j // 4)
                want = wanted(axis, line, lax.rem(j, 4))
                near = (want[0] == u) | (want[0] == mod4(u + (-1 if role == 0 else 1)))
                mine = relays[k][entry_of(role, u, want)]
                other = swaps[k][role * 8 + j]
                sends[k][role * 8 + j] = jnp.where(near, mine, other)
        for role in range(2):
            own_part(k, role).start()

    def deliver(pair):
        for k in pair:
            deliver_pick(k)
        for i, (dv, role, line) in enumerate(LAST):
            for k in pair:
                axis = CHUNKS[k][4]
                u, v = place_of(axis)
                r = mod4(v + dv)
                to = dev_of(axis, mod4(u + line - (1 if role == 0 else 0)), r)
                remote(
                    sends[k].at[role * 8 + line * 4 + r], landing(k, role), sem_3s.at[k], sem_3r.at[k, i], (g, to)
                ).start()

    def own_part(k, role):
        return pltpu.make_async_copy(
            sends[k].at[own_slot(CHUNKS[k][4], role)], landing(k, role), sem_own3.at[k, role]
        )

    sm.wait()

    meta_own.wait()
    wait_recv_all(meta_rx.at[pl.ds(0, ND - 1)], sem_meta.at[1])
    mine_w = place[0]
    got = meta_rx[lax.rem(mine_w // HOLD, ND)]
    slot_m = lax.rem(mine_w, HOLD)
    got_wide = got.astype(F32)
    mine_scales = jnp.where(slot_m == 0, got_wide[0:8], got_wide[8:16])
    scale_out[...] = mine_scales[:, 0:KT].astype(BF)

    def grow_scales(block, m, f):
        tiles = 2 * (iota((128, HALF), 1) // TILE) + f
        sel = (iota((128, HALF), 0) == tiles + 8 * m).astype(BF)
        tall = jnp.concatenate([block.astype(F32), jnp.zeros((112, 128), F32)], axis=0).T
        return jnp.dot(tall[0:32].astype(BF), sel, preferred_element_type=F32).reshape(32, 1, HALF)

    for f in range(2):
        for m in range(HOLD):
            grow[m, f] = grow_scales(meta_tx[...], m, f)
        grow[HOLD, f] = grow_scales(got, slot_m, f)

    tok_own.wait()
    wait_recv_all(rx.at[pl.ds(0, ND - 1)], sem_tok2.at[1])

    pack_rows(rx, big, True)

    code = big[:, D:]
    load_row = jnp.zeros((1, 128), F32)
    for s in range(HOLD + 1):
        count = jnp.sum(jnp.where(code == float(s), 1.0, 0.0), axis=0, keepdims=True)
        load_row = jnp.where(iota((1, 128), 1) == s, count, load_row)
    load_out[...] = load_row[:, 0 : HOLD + 1].astype(I32)

    for s in range(HOLD + 1):
        @pl.loop(0, KT)
        def _(k, s=s):
            cols = pl.ds(pl.multiple_of(k * TILE, TILE), TILE)
            xm[s, :, cols] = jnp.where(code == float(s), big[:, cols], 0.0).astype(BF)

    acc[...] = jnp.zeros((2, CELLS, HALF), F32)
    n_q = HOLD * (D // QROWS)

    @pl.loop(0, n_q)
    def _(i):
        @pl.when(i + 1 < n_q)
        def _():
            q_copy(i + 1).start()
        q_copy(i).wait()
        m = i // (D // QROWS)
        tile0 = lax.rem(i, D // QROWS) * (QROWS // TILE)
        xs = xm[m, :, pl.ds(pl.multiple_of(tile0 * TILE, TILE), QROWS)]
        for f in range(2):
            cols = [qbuf[lax.rem(i, 2), :, 256 * r + 128 * f : 256 * r + 128 * f + 128] for r in range(4)]
            w = jnp.concatenate(cols, axis=1).astype(F32).reshape(QROWS // TILE, TILE, HALF)
            w = (w * grow[m, f, pl.ds(tile0, QROWS // TILE)]).astype(BF).reshape(QROWS, HALF)
            acc[f] += jnp.dot(xs, w, preferred_element_type=F32)

    trade((0, 1))
    trade((2, 3))
    deliver((0, 1))
    deliver((2, 3))

    def serve_part(k, c, r):
        f, _, base, rows, _ = CHUNKS[k]
        at = piece_rows(c, base, rows)
        tiles = pl.ds(c * (PIECE // TILE) + base // TILE, rows // TILE)
        cols = pl.ds(pl.multiple_of(r * 128, 128), 128)
        w = w_new[at, piece_cols(r, f)].astype(F32).reshape(rows // TILE, TILE, 128)
        w = (w * grow[HOLD, f, tiles, :, cols]).astype(BF).reshape(rows, 128)
        acc[f, :, cols] += jnp.dot(xm[HOLD, :, at], w, preferred_element_type=F32)

    def serve_own(pair):
        for k in pair:
            u, v = place_of(CHUNKS[k][4])
            for role in range(2):
                own_part(k, role).wait()
                serve_part(k, u if role == 0 else mod4(u - 1), v)

    def serve(pair, lo, hi):
        for i, (dv, role, line) in list(enumerate(LAST))[lo:hi]:
            for k in pair:
                u, v = place_of(CHUNKS[k][4])
                got = w_new.at[pl.ds(0, CHUNKS[k][3]), pl.ds(0, 128)]
                pltpu.make_async_copy(got, got, sem_3r.at[k, i]).wait()
                c = mod4(u - line + (1 if role == 0 else -1))
                serve_part(k, c, mod4(v - dv))

    def back_rows(p):
        return pl.ds(pl.multiple_of(p * NG, NG), NG)

    def finish(f):
        v = acc[f]
        acc[f] = v / (1.0 + jnp.exp(-v))
        peers = [peer(o) for o in ORDER] + [d]
        for i, p in enumerate(peers):
            unpack_part(acc.at[f], back_tx.at[f], p)
            if i > 0:
                back_send(f, peers[i - 1])
        back_copy(f).start()

    def back_send(f, p):
        remote(
            back_tx.at[f, back_rows(p)], back_mid.at[f, :, d], sem_ret.at[f, 0], sem_ret.at[f, 1], (g, p)
        ).start()

    def back_copy(f):
        return pltpu.make_async_copy(back_tx.at[f, back_rows(d)], back_mid.at[f, :, d], sem_local.at[5 + f])

    def back_own(f):
        return pltpu.make_async_copy(back_mid.at[f, g], back_rx.at[f, group_rows], sem_local.at[9 + f])

    def back_across(f):
        back_copy(f).wait()
        wait_recv_all(back_mid.at[f, :, pl.ds(0, ND - 1)], sem_ret.at[f, 1])
        for i in range(1, NG):
            t = across(i)
            remote(
                back_mid.at[f, t], back_rx.at[f, group_rows], sem_ret2.at[f, 0], sem_ret2.at[f, 1], (t, d)
            ).start()
        back_own(f).start()

    def arrive(f):
        back_own(f).wait()
        wait_recv_all(back_rx.at[f, pl.ds(0, ND * (NG - 1))], sem_ret2.at[f, 1])
        pack_rows(back_rx.at[f], acc.at[f])
        part = jnp.dot(placed_t[...], acc[f].astype(BF), preferred_element_type=F32)
        part = (part * weight_col[:, 0:1]).astype(BF)
        for r in range(4):
            hidden_out[:, 256 * r + 128 * f : 256 * r + 128 * f + 128] = part[:, 128 * r : 128 * r + 128]

    serve_own((0, 1))
    serve((0, 1), 0, 14)
    finish(0)
    serve_own((2, 3))
    serve((2, 3), 0, 14)
    finish(1)
    back_across(0)
    back_across(1)
    arrive(0)
    arrive(1)

    wait_recv_all(place_rx.at[pl.ds(0, ND - 1)], sem_place.at[0])
    wait_recv_all(place_rx.at[pl.ds(0, ND * (NG - 1))], sem_spread.at[0])
    wait_recv_all(meta_rx.at[pl.ds(0, ND - 1)], sem_meta.at[0])
    for k in range(4):
        wait_recv_all(relays[k].at[pl.ds(0, 28)], sem_1s.at[k])
        wait_recv_all(sends[k].at[pl.ds(0, 14)], sem_3s.at[k])
    wait_recv_all(mid.at[pl.ds(0, NG - 1)], sem_tok.at[0])
    wait_recv_all(rx.at[pl.ds(0, ND - 1)], sem_tok2.at[0])
    for f in range(2):
        wait_recv_all(back_mid.at[f, :, pl.ds(0, ND - 1)], sem_ret.at[f, 0])
        wait_recv_all(back_rx.at[f, pl.ds(0, ND * (NG - 1))], sem_ret2.at[f, 0])


def store(w, scale, hidden, load, w_out, scale_out, hidden_out, load_out, sems):
    n = 4
    part = D // n
    copies = [
        pltpu.make_async_copy(w.at[pl.ds(i * part, part)], w_out.at[pl.ds(i * part, part)], sems.at[i]) for i in range(n)
    ]
    for i, (a, b) in enumerate(((scale, scale_out), (hidden, hidden_out), (load, load_out))):
        copies.append(pltpu.make_async_copy(a, b, sems.at[n + i]))
    for c in copies:
        c.start()
    for c in copies:
        c.wait()


def per_device(primary_q, primary_scales, new_place, tokens, experts, replica, route_num):
    vmem = pl.BlockSpec(memory_space=pltpu.VMEM)
    anywhere = pl.BlockSpec(memory_space=pl.ANY)
    dma = pltpu.SemaphoreType.DMA
    scratch = [
        pltpu.VMEM((1, 128), I32),
        pltpu.VMEM((N, 1, 128), I32),
        pltpu.SMEM((ND, 1, 128), I32),
        pltpu.VMEM((16, 128), BF),
        pltpu.VMEM((ND, 16, 128), BF),
        *[pltpu.VMEM((32, c[3], 128), BF) for c in CHUNKS],
        *[pltpu.VMEM((16, c[3], 128), BF) for c in CHUNKS],
        *[pltpu.VMEM((16, c[3], 128), BF) for c in CHUNKS],
        pltpu.VMEM((CELLS, WIDE), F32),
        pltpu.VMEM((N, CAP, WIDE), BF),
        pltpu.VMEM((NG, ND, CAP, WIDE), BF),
        pltpu.VMEM((ND, NG, CAP, WIDE), BF),
        pltpu.VMEM((HOLD + 1, CELLS, D), BF),
        pltpu.VMEM((2, CELLS, HALF), F32),
        pltpu.VMEM((2, N, CAP, HALF), BF),
        pltpu.VMEM((2, NG, ND, CAP, HALF), BF),
        pltpu.VMEM((2, N, CAP, HALF), BF),
        pltpu.VMEM((2, QROWS, FF), BF),
        pltpu.VMEM((HOLD + 1, 2, 32, 1, HALF), F32),
        pltpu.VMEM((PAIRS, CELLS), BF),
        dma((2,)), dma((2,)), dma((2,)), dma((4,)), dma((4,)), dma((4,)), dma((4,)), dma((4,)), dma((4, 14)),
        dma((4, 2)), dma((4, 2)),
        dma((2,)), dma((2,)), dma((2, 2)), dma((2, 2)), dma((11,)), dma((2,)),
    ]
    new_weights, scale_tile, hidden, load = pl.pallas_call(
        kernel,
        out_shape=(
            pltpu.VMEM((D, FF), BF),
            pltpu.VMEM((8, KT), BF),
            pltpu.VMEM((PAIRS, FF), BF),
            pltpu.VMEM((1, HOLD + 1), I32),
        ),
        in_specs=[
            anywhere, vmem, pl.BlockSpec(memory_space=pltpu.SMEM), vmem, vmem, vmem, vmem,
        ],
        out_specs=(vmem, vmem, vmem, vmem),
        scratch_shapes=scratch,
        compiler_params=pltpu.CompilerParams(
            collective_id=0, has_side_effects=True, vmem_limit_bytes=56000 * 1024
        ),
    )(
        primary_q, primary_scales.transpose(0, 2, 1), new_place, tokens,
        experts.T, replica.T, route_num.T,
    )
    results = [
        pltpu.with_memory_space_constraint(a, pltpu.VMEM) for a in (new_weights, scale_tile, hidden, load)
    ]
    new_weights, scale_tile, hidden, load = pl.pallas_call(
        store,
        out_shape=(
            jax.ShapeDtypeStruct((D, FF), BF),
            jax.ShapeDtypeStruct((8, KT), BF),
            jax.ShapeDtypeStruct((PAIRS, FF), BF),
            jax.ShapeDtypeStruct((1, HOLD + 1), I32),
        ),
        in_specs=[vmem] * 4,
        out_specs=(anywhere,) * 4,
        scratch_shapes=[dma((7,))],
        compiler_params=pltpu.CompilerParams(vmem_limit_bytes=1024 * 1024),
    )(*results)
    return (
        new_weights.reshape(1, D, FF),
        scale_tile.T.reshape(1, KT, 8),
        hidden.reshape(ROWS, TOPK, FF),
        load,
    )


def solution(mesh):
    both = ("group", "dev")
    return jax.shard_map(
        per_device,
        mesh=mesh,
        in_specs=(
            P(both, None, None), P(both, None, None), P(both), P(both, None),
            P(both, None), P(both, None), P(both, None),
        ),
        out_specs=(P(both, None, None), P(both, None, None), P(both, None, None), P(both, None)),
        check_vma=False,
    )
```
